128 devices in a mesh: expert: 64 (over z, y, x), dp: 2 (over core).
Axes of the slice: x: 4, y: 4, z: 4, core: 2. Of those that a mesh axis runs over, the one named last changes fastest.
Arguments:
- tokens: bfloat16 [8192, 2048], P(('expert', 'dp')), may hold values from -6 to 6
- grad_out: bfloat16 [8192, 2048], P(('expert', 'dp')), may hold values from -6 to 6
- expert_ids: int32 [8192, 8], P(('expert', 'dp')), may hold values from 0 to 63, all different within a row; in each aligned block of 64 rows (0 to 63, 64 to 127, ...) at most 12 rows name the same one
- router_weights: float32 [8192, 8], P(('expert', 'dp')), may hold values from 0.02 to 0.25
- codes_in: int32 [64, 2, 2048, 256], P('expert', None, 'dp'), may hold values from 0 to 4095
- codes_out: int32 [64, 256, 2048], P('expert', None, 'dp'), may hold values from 0 to 4095
- clip_in: float32 [64, 2, 2, 16, 768], P('expert'), may hold values from -1 to 3
- range_in: float32 [64, 2, 2, 16, 768], P('expert'), may hold values from 0.01 to 0.06
- clip_out: float32 [64, 2, 6, 2048], P('expert'), may hold values from -1 to 3
- range_out: float32 [64, 2, 6, 2048], P('expert'), may hold values from 0.018 to 0.1
Outputs:
- grad_tokens: bfloat16 [8192, 2048], P(('expert', 'dp'))
- grad_clip_in: float32 [64, 2, 2, 16, 768], P('expert', None, None, 'dp')
- grad_clip_out: float32 [64, 2, 6, 2048], P('expert', None, None, 'dp')
The draws below stay inside these ranges and needn't reach their ends.
Inputs may be any that keep to these rules, and one draw needn't show every extreme that they name: `expert_ids`: each row names 8 different experts; among the rows of one device no expert is named by more than 12 rows, and in some device some expert is named by exactly 12 rows.
All inputs are finite; a program needn't handle non-finite values.
Results may differ from the reference program's by a relative error of at most 0.0082.
Values may be sent and summed in bfloat16 or wider, within the bound.
A program may use at most 128 MiB of HBM per device.

```python
import math
import jax
import jax.numpy as jnp
import numpy as np
from jax import lax

D = 2048
FF = 768
TOP = 8
GROUP = 128
TOK_DEV = 64
EXPERTS = 64
CAP = 12
TOKENS = 8192
G_IN = 16
G_OUT = 6


def plant(array, key, least, high):
    longest = array.shape.index(max(array.shape))
    spots = []
    for shift in (0, 1):
        where = [jax.random.randint(jax.random.fold_in(key, axis), (), 0, length) for axis, length in enumerate(array.shape)]
        where[longest] = (where[longest] + shift) % array.shape[longest]
        spots.append(tuple(where))
    return array.at[spots[0]].set(least).at[spots[1]].set(high)


def block_scale(stream_key, dims, shards, smallest, high):
    gain = 1.0
    for position, blocks in shards:
        heights = jax.random.uniform(jax.random.fold_in(jax.random.fold_in(stream_key, 6), position), (blocks,), jnp.float32, smallest / len(shards), high / len(shards))
        gain = gain * jnp.repeat(jnp.exp(heights), dims[position] // blocks).reshape((-1,) + (1,) * (len(dims) - 1 - position))
    return gain


def deal_out(key, own, number, rows, amount, top, limit, lean):
    ranking = jax.random.permutation(key, amount)
    heavy_load, common = portions_of(amount, rows * top, limit, lean, True), portions_of(amount, rows * top, limit, lean, False)
    places = jnp.arange(amount)

    def named(sizes, offset_by):
        used = int((sizes > 0).sum())
        fixed = max(1, used // 4)
        passed = fixed + (places - fixed + offset_by * (used - fixed)) % max(1, amount - fixed)
        return jnp.zeros((amount,), jnp.int32).at[ranking[jnp.where(places < fixed, places, passed)]].set(jnp.asarray(sizes, jnp.int32))

    sizes = jnp.where(number % 4 == 0, named(heavy_load, number // 4), named(common, number - number // 4 - 1))
    mixed = jax.random.permutation(jax.random.fold_in(own, 3), amount)
    donor, sink = mixed[0:amount // 2 * 2:2], mixed[1:amount // 2 * 2:2]
    margin = jnp.minimum(sizes[donor] - 1, limit - sizes[sink]) // 2
    margin = jnp.where((donor == ranking[0]) | (sink == ranking[0]) | (sizes[sink] == 0), 0, jnp.maximum(margin, 0))
    passed = jax.random.randint(jax.random.fold_in(own, 4), (amount // 2,), 0, 1 << 20) % (margin + 1)
    sizes = sizes.at[donor].add(-passed).at[sink].add(passed)
    labels = jnp.searchsorted(jnp.cumsum(sizes), jnp.arange(rows * top), side="right").astype(jnp.int32)
    listing = labels.reshape(top, rows).T
    listing = listing[jax.random.permutation(jax.random.fold_in(own, 1), rows)]
    offset_by = jax.random.randint(jax.random.fold_in(own, 2), (rows, 1), 0, top)
    return jnp.take_along_axis(listing, (jnp.arange(top)[None, :] + offset_by) % top, axis=1)


def portions_of(number_of, total, limit, skew, full):
    weights = [(1 << 20) // math.isqrt(grade ** skew) + 1 for grade in range(1, number_of + 1)]
    largest = limit if full else min(limit, max(-(-total // number_of), total * weights[0] // sum(weights)))
    least = 1 if total - largest >= number_of - 1 else 0
    given, spare = [largest] + [least] * (number_of - 1), total - largest - least * (number_of - 1)
    while spare > 0:
        movable = [i for i in range(1, number_of) if given[i] < largest] or [i for i in range(1, number_of) if given[i] < limit]
        whole, left = sum([weights[i] for i in movable]), spare
        for i in movable:
            extra = min(limit - given[i], max(1, left * weights[i] // whole), spare)
            given[i] = given[i] + extra
            spare = spare - extra
    return np.array(given)


def gaussian(key, extent, scale, most, cuts=(), kind=jnp.bfloat16):
    entries = scale * jax.random.normal(key, extent, jnp.float32)
    if cuts:
        entries = entries * block_scale(key, extent, cuts, -0.22, 0.18)
    return jnp.clip(entries, -most, most).astype(kind)


def setup_inputs(seed: int = 0) -> dict:
    key_list = jax.random.split(jax.random.key(seed), 11)
    tokens = gaussian(key_list[0], (TOKENS, D), 1.0, 6.0, ((0, 128),))
    grad_out = gaussian(key_list[1], (TOKENS, D), 1.0, 6.0, ((0, 128),))
    expert_ids_keys = jax.random.split(jax.random.fold_in(key_list[2], 1), TOKENS // TOK_DEV)
    expert_ids_turns = jax.random.permutation(jax.random.fold_in(key_list[2], 3), TOKENS // TOK_DEV)
    expert_ids = jax.vmap(lambda own, number: deal_out(jax.random.fold_in(key_list[2], 2), own, number, TOK_DEV, EXPERTS, TOP, CAP, 2))(expert_ids_keys, expert_ids_turns).reshape((TOKENS, TOP))
    router_weights = jnp.clip(0.02 + 0.23 * jax.random.uniform(key_list[3], (TOKENS, TOP), jnp.float32) ** block_scale(key_list[3], (TOKENS, TOP), ((0, 128),), -0.2, 0.2), 0.02, 0.25)
    codes_in = plant(jax.random.randint(key_list[4], (EXPERTS, 2, D, FF // 3), 0, 4096), jax.random.fold_in(key_list[4], 1), 0, 4095).astype(jnp.int32)
    codes_out = plant(jax.random.randint(key_list[5], (EXPERTS, FF // 3, D), 0, 4096), jax.random.fold_in(key_list[5], 1), 0, 4095).astype(jnp.int32)
    clip_in = jnp.clip(-1.0 + 4.0 * jax.random.uniform(key_list[6], (EXPERTS, 2, 2, G_IN, FF), jnp.float32) ** block_scale(key_list[6], (EXPERTS, 2, 2, G_IN, FF), ((0, 64),), -0.2, 0.2), -1.0, 3.0)
    range_in = jnp.clip(jnp.exp(math.log(0.06) - 1.7917595 * jax.random.uniform(key_list[7], (EXPERTS, 2, 2, G_IN, FF), jnp.float32) ** block_scale(key_list[7], (EXPERTS, 2, 2, G_IN, FF), ((0, 64),), -0.2, 0.2)), 0.01, 0.06)
    clip_out = jnp.clip(-1.0 + 4.0 * jax.random.uniform(key_list[8], (EXPERTS, 2, G_OUT, D), jnp.float32) ** block_scale(key_list[8], (EXPERTS, 2, G_OUT, D), ((0, 64),), -0.2, 0.2), -1.0, 3.0)
    range_out = jnp.clip(jnp.exp(math.log(0.1) - 1.7147985 * jax.random.uniform(key_list[9], (EXPERTS, 2, G_OUT, D), jnp.float32) ** block_scale(key_list[9], (EXPERTS, 2, G_OUT, D), ((0, 64),), -0.2, 0.2)), 0.018, 0.1)
    return dict(tokens=tokens, grad_out=grad_out, expert_ids=expert_ids, router_weights=router_weights, codes_in=codes_in, codes_out=codes_out, clip_in=clip_in, range_in=range_in, clip_out=clip_out, range_out=range_out)


def unpack_columns(packed):
    shifts = 4 * jnp.arange(3, dtype=jnp.int32)
    nibble = jnp.bitwise_and(jnp.right_shift(packed[..., None], shifts), 15)
    new_shape = packed.shape[:-1] + (packed.shape[-1] * 3,)
    return nibble.reshape(new_shape).astype(jnp.bfloat16)


def unpack_rows(packed):
    shifts = 4 * jnp.arange(3, dtype=jnp.int32)
    nibble = jnp.bitwise_and(jnp.right_shift(packed[:, None, :], shifts[:, None]), 15)
    return nibble.reshape(packed.shape[0] * 3, packed.shape[1]).astype(jnp.bfloat16)


def dequantize(code_rows, clip_pair, range_pair):
    upper_end = jax.nn.sigmoid(clip_pair[0]) * range_pair[0]
    lower_end = jax.nn.sigmoid(clip_pair[1]) * range_pair[1]
    step_size = (upper_end + lower_end) / 15.0
    groups = code_rows.shape[0] // GROUP
    blocked = code_rows.reshape(groups, GROUP, code_rows.shape[1])
    weight = step_size[:, None, :] * blocked - lower_end[:, None, :]
    return weight.reshape(code_rows.shape).astype(jnp.bfloat16)


def group_terms(grad_weight, weight, clip_pair, range_pair):
    upper_end = jax.nn.sigmoid(clip_pair[0]) * range_pair[0]
    lower_end = jax.nn.sigmoid(clip_pair[1]) * range_pair[1]
    groups = grad_weight.shape[0] // GROUP
    blocked = grad_weight.reshape(groups, GROUP, grad_weight.shape[1])
    shifted = weight.astype(jnp.float32).reshape(blocked.shape) + lower_end[:, None, :]
    weighted = jnp.sum(blocked * shifted, axis=1) / (upper_end + lower_end)
    return jnp.stack([weighted, weighted - jnp.sum(blocked, axis=1)])


def clip_grads(group_sums, clip_pair, range_pair):
    sig_upper = jax.nn.sigmoid(clip_pair[0])
    sig_lower = jax.nn.sigmoid(clip_pair[1])
    return jnp.stack([group_sums[0] * range_pair[0] * sig_upper * (1.0 - sig_upper),
                      group_sums[1] * range_pair[1] * sig_lower * (1.0 - sig_lower)])


def contract(left_side, right_side, left_dim, right_dim):
    return lax.dot_general(left_side, right_side, (((left_dim,), (right_dim,)), ((), ())),
                           preferred_element_type=jnp.float32)


def expert_forward(token_rows, gate_weight, up_weight):
    gate_pre = jnp.dot(token_rows, gate_weight, preferred_element_type=jnp.float32)
    up_pre = jnp.dot(token_rows, up_weight, preferred_element_type=jnp.float32)
    gate_sig = jax.nn.sigmoid(gate_pre)
    gate_act = gate_pre * gate_sig
    hidden = (gate_act * up_pre).astype(jnp.bfloat16)
    return gate_pre, up_pre, gate_sig, gate_act, hidden


def expert_backward(forward_parts, slope_rows, gate_weight, up_weight, down_weight):
    gate_pre, up_pre, gate_sig, gate_act, hidden = forward_parts
    grad_hidden = contract(slope_rows, down_weight, 1, 1)
    grad_gate = (grad_hidden * up_pre * gate_sig * (1.0 + gate_pre * (1.0 - gate_sig))).astype(jnp.bfloat16)
    grad_up = (grad_hidden * gate_act).astype(jnp.bfloat16)
    grad_rows = (contract(grad_gate, gate_weight, 1, 1) + contract(grad_up, up_weight, 1, 1)).astype(jnp.bfloat16)
    return grad_gate, grad_up, grad_rows


def reference(tokens, grad_out, expert_ids, router_weights, codes_in, codes_out, clip_in, range_in, clip_out, range_out):
    blocks = TOKENS // TOK_DEV
    assign = TOK_DEV * TOP
    flat_ids = expert_ids.reshape(blocks, assign)
    onehot = (flat_ids[:, :, None] == jnp.arange(EXPERTS, dtype=jnp.int32)[None, None, :]).astype(jnp.int32)
    before = jnp.sum((jnp.cumsum(onehot, axis=1) - onehot) * onehot, axis=2)
    block_idx = jnp.arange(blocks, dtype=jnp.int32)[:, None] * jnp.ones((1, assign), jnp.int32)
    token_row = block_idx * TOK_DEV + (jnp.arange(assign, dtype=jnp.int32) // TOP)[None, :]
    slot_token = jnp.full((blocks, EXPERTS, CAP), -1, jnp.int32).at[block_idx, flat_ids, before].set(token_row)
    slot_weight = jnp.zeros((blocks, EXPERTS, CAP), jnp.float32).at[block_idx, flat_ids, before].set(
        router_weights.reshape(blocks, assign))

    def per_expert(running, expert):
        code_in = unpack_columns(codes_in[expert])
        code_out = unpack_rows(codes_out[expert])
        gate_weight = dequantize(code_in[0], clip_in[expert, 0], range_in[expert, 0])
        up_weight = dequantize(code_in[1], clip_in[expert, 1], range_in[expert, 1])
        down_weight = dequantize(code_out, clip_out[expert], range_out[expert])
        slot_rows = slot_token[:, expert, :].reshape(-1)
        is_live = slot_rows >= 0
        safe_rows = jnp.maximum(slot_rows, 0)
        token_rows = jnp.where(is_live[:, None], tokens[safe_rows], jnp.zeros((), jnp.bfloat16))
        route_scale = slot_weight[:, expert, :].reshape(-1)
        slope_rows = (route_scale[:, None] * grad_out[safe_rows].astype(jnp.float32)).astype(jnp.bfloat16)
        forward_parts = expert_forward(token_rows, gate_weight, up_weight)
        grad_gate, grad_up, grad_rows = expert_backward(forward_parts, slope_rows, gate_weight, up_weight, down_weight)
        running = running.at[safe_rows].add(grad_rows.astype(jnp.float32))
        sums_in = jnp.stack([group_terms(contract(token_rows, grad_gate, 0, 0), gate_weight, clip_in[expert, 0], range_in[expert, 0]),
                             group_terms(contract(token_rows, grad_up, 0, 0), up_weight, clip_in[expert, 1], range_in[expert, 1])])
        sums_out = group_terms(contract(forward_parts[4], slope_rows, 0, 0), down_weight, clip_out[expert], range_out[expert])
        out_in = jnp.stack([clip_grads(sums_in[0], clip_in[expert, 0], range_in[expert, 0]),
                            clip_grads(sums_in[1], clip_in[expert, 1], range_in[expert, 1])])
        out_out = clip_grads(sums_out, clip_out[expert], range_out[expert])
        return running, (out_in, out_out)

    running, (grad_clip_in, grad_clip_out) = lax.scan(
        per_expert, jnp.zeros((TOKENS, D), jnp.float32), jnp.arange(EXPERTS, dtype=jnp.int32))
    return running.astype(jnp.bfloat16), grad_clip_in, grad_clip_out
```

```python
import functools

import jax
import jax.numpy as jnp
from jax import lax
from jax.experimental import pallas as pl
from jax.experimental.pallas import tpu as pltpu
from jax.sharding import PartitionSpec as P

MESH = pl.DeviceIdType.MESH
D, FF, TOK = 2048, 768, 64
WIDTH = (640, 640, 768)
FIRST = (0, 640, 1280)
BF, F32, I32 = jnp.bfloat16, jnp.float32, jnp.int32
HI = lax.Precision.HIGHEST


def dot(a, b, da, db, **kw):
    return lax.dot_general(a, b, (((da,), (db,)), ((), ())), preferred_element_type=F32, **kw)


def iota(shape, dim):
    return lax.broadcasted_iota(I32, shape, dim)


def sigmoid(v):
    return 1.0 / (1.0 + jnp.exp(-v))


def down_blocks():
    out = []
    for k in range(3):
        for block in range(8):
            rows = range(block * 32, block * 32 + 32)
            groups = {}
            for r in rows:
                groups.setdefault((3 * r + k) // 128, []).append(r - block * 32)
            out.append((k, block * 32, [(g, min(v), max(v) + 1) for g, v in sorted(groups.items())]))
    return out


def kernel(
    tok, go, ids, rw, cin, cout, clin, rgin, clout, rgout,
    o_tok, o_in, o_out,
    posw, t4a, t4b, t4c, g4a, g4b, g4c, pw4,
    sta, stb, stc, ssa, ssb, ssc,
    x5, d5, g5, xeb, xec, deb, dec, geb, gec, ra, rb, rc, p4s,
    wgu, wd, upgu, logu, upo, loo,
    hid, ggu, fac, act, qa, qb, qc, ha, hb, hc,
    sbi, sbo, rbi, rbo,
    ag_s, ag_r, pw_s, pw_r, sl_s, sl_r, sl_l, rt_s, rt_r, rt_l, pt_s, pt_r, wt_s, wt_r, sm_s, sm_r,
):
    e, d = lax.axis_index("expert"), lax.axis_index("dp")
    z, y, x = e // 16, (e // 4) % 4, e % 4
    here = (x, y, z)
    t4, g4 = (t4a, t4b, t4c), (g4a, g4b, g4c)
    st, ss = (sta, stb, stc), (ssa, ssb, ssc)
    xe, de, ge = (None, xeb, xec), (None, deb, dec), (None, geb, gec)
    rr, part, got = (ra, rb, rc), (qa, qb, qc), (ha, hb, hc)
    cols = [pl.ds(FIRST[c], WIDTH[c]) for c in range(3)]

    def expert_at(zz, yy, xx):
        return zz * 16 + yy * 4 + xx

    def line_peer(c, k):
        s = (here[c] + k) % 4
        return s, (expert_at(z, y, s), expert_at(z, s, x), expert_at(s, y, x))[c]

    def plane_peer(c, o):
        a, b = o // 4, o % 4
        u, v = ((z, y), (z, x), (y, x))[c]
        u, v = (u + a) % 4, (v + b) % 4
        return u, v, (expert_at(u, v, x), expert_at(u, y, v), expert_at(z, u, v))[c]

    def main_rows(ref, c, u, v):
        if c == 0:
            return ref.at[u, v, :, :, cols[c]]
        if c == 1:
            return ref.at[u, :, v, :, cols[c]]
        return ref.at[pl.ds(0, 4), u, v, :, cols[c]]

    def extra_rows(ref, sides, c, u, v):
        if c == 0:
            return ref.at[4 + u // 2, (u % 2) * 2 + v // 2, pl.ds((v % 2) * 2, 2), :, cols[c]]
        return sides[c].at[u * 4 + v]

    def remote(src, dst, s, r, who, core):
        return pltpu.make_async_remote_copy(
            src_ref=src, dst_ref=dst, send_sem=s, recv_sem=r, device_id=(who, core), device_id_type=MESH
        )

    def wait_bytes(ref, sem):
        pltpu.make_async_copy(ref, ref, sem).wait()

    plane_me = (z * 4 + y, z * 4 + x, y * 4 + x)
    plane_uv = ((z, y), (z, x), (y, x))

    barrier = pltpu.get_barrier_semaphore()

    def greet(o, carry):
        pl.semaphore_signal(barrier, inc=1, device_id=((e + o) % 64, d), device_id_type=MESH)
        return carry

    lax.fori_loop(1, 64, greet, 0)
    pl.semaphore_signal(barrier, inc=1, device_id=(e, 1 - d), device_id_type=MESH)

    lane = iota((TOK, 128), 1)
    chosen = jnp.zeros((TOK, 128), F32)
    weight = jnp.zeros((TOK, 128), F32)
    for k in range(8):
        ident = ids[:, k : k + 1]
        chosen = chosen + jnp.where(lane == ident, 1.0, 0.0)
        weight = weight + jnp.where(lane == ident + 64, rw[:, k : k + 1], 0.0)
    lower_tri = jnp.where(iota((TOK, TOK), 0) > iota((TOK, TOK), 1), 1.0, 0.0).astype(BF)
    before = dot(lower_tri, chosen.astype(BF), 1, 0)
    posw[...] = jnp.where(chosen > 0.5, before, -64.0 * jnp.where(lane < 64, 1.0, 0.0)) + weight
    for c in range(3):
        pw4[c, here[c]] = posw[...]
        t4[c][here[c]] = tok[:, cols[c]]
        g4[c][here[c]] = go[:, cols[c]]

    pl.semaphore_wait(barrier, 64)

    for k in (2, 1, 3):
        for c in range(3):
            _, who = line_peer(c, k)
            remote(posw, pw4.at[c, here[c]], pw_s.at[c], pw_r.at[c], who, d).start()
            remote(tok.at[:, cols[c]], t4[c].at[here[c]], ag_s.at[0, c], ag_r.at[0, c], who, d).start()
    for k in (2, 1, 3):
        for c in range(3):
            _, who = line_peer(c, k)
            remote(go.at[:, cols[c]], g4[c].at[here[c]], ag_s.at[1, c], ag_r.at[1, c], who, d).start()

    perm = jnp.where(
        iota((FF, FF), 0) == 3 * (iota((FF, FF), 1) & 255) + (iota((FF, FF), 1) >> 8), 1.0, 0.0
    )
    for p in range(2):
        up = sigmoid(clin[p, 0]) * rgin[p, 0]
        lo = sigmoid(clin[p, 1]) * rgin[p, 1]
        upgu[:, p * FF : (p + 1) * FF] = dot(up, perm, 1, 0, precision=HI)
        logu[:, p * FF : (p + 1) * FF] = dot(lo, perm, 1, 0, precision=HI)
    upo[...] = sigmoid(clout[0]) * rgout[0]
    loo[...] = sigmoid(clout[1]) * rgout[1]

    def dequant_in(g, carry):
        up = upgu[pl.ds(d * 8 + g, 1), :]
        lo = logu[pl.ds(d * 8 + g, 1), :]
        step = (up + lo) / 15.0
        for p in range(2):
            words = cin[p, pl.ds(g * 128, 128), :]
            for k in range(3):
                c0 = p * FF + k * 256
                code = ((words >> (4 * k)) & 15).astype(F32)
                wgu[pl.ds(d * 1024 + g * 128, 128), c0 : c0 + 256] = (
                    code * step[:, c0 : c0 + 256] - lo[:, c0 : c0 + 256]
                ).astype(BF)
        return carry

    lax.fori_loop(0, 8, dequant_in, 0)
    half = pl.ds(pl.multiple_of(d * 1024, 1024), 1024)
    up_half, lo_half = upo[:, half], loo[:, half]
    step_half = (up_half + lo_half) / 15.0
    for k, r0, groups in down_blocks():
        code = ((cout[r0 : r0 + 32, :] >> (4 * k)) & 15).astype(F32)
        row = iota((32, 1024), 0)
        scale, shift = step_half[groups[0][0]][None], lo_half[groups[0][0]][None]
        for g, first, _ in groups[1:]:
            scale = jnp.where(row >= first, step_half[g][None], scale)
            shift = jnp.where(row >= first, lo_half[g][None], shift)
        wd[k * 256 + r0 : k * 256 + r0 + 32, half] = (code * scale - shift).astype(BF)

    other = 1 - d
    wgu_half = wgu.at[pl.ds(pl.multiple_of(d * 1024, 1024), 1024), :]
    wd_half = wd.at[:, half]
    remote(wgu_half, wgu_half, wt_s.at[0], wt_r.at[0], e, other).start()
    remote(wd_half, wd_half, wt_s.at[1], wt_r.at[1], e, other).start()

    def selector(c, first):
        q = iota((16, 48, 128), 0)
        u, v = q >> 2, q & 3
        target = (u * 16 + v * 4 + x, u * 16 + y * 4 + v, z * 16 + u * 4 + v)[c]
        return jnp.where(iota((16, 48, 128), 2) == target + first, 1.0, 0.0).reshape(768, 128)

    r = iota((16, 48, 256), 1)
    tail = r - 32
    wanted = jnp.where(r < 32, (r >> 3) * 16 + (r & 7), (tail >> 2) * 16 + 8 + (tail & 3))
    source = iota((16, 48, 256), 2) >> 6
    wanted = (wanted - 16 * source).astype(F32).reshape(768, 256)

    def send_slots(s, x_to, sides, c, t):
        def one(i, carry):
            o = jnp.where(i < 6, 10 + i, i - 5)
            u, v, who = plane_peer(c, o)
            q = u * 4 + v
            mu, mv = plane_uv[c]
            remote(s.at[q, pl.ds(0, 4)], main_rows(x_to, c, mu, mv), sl_s.at[t, c], sl_r.at[t, c], who, d).start()
            remote(s.at[q, pl.ds(4, 2)], extra_rows(x_to, sides, c, mu, mv), sl_s.at[t, c], sl_r.at[t, c], who, d).start()
            return carry

        lax.fori_loop(0, 15, one, 0)
        q = plane_me[c]
        mu, mv = plane_uv[c]
        pltpu.make_async_copy(s.at[q, pl.ds(0, 4)], main_rows(x_to, c, mu, mv), sl_l.at[t, c]).start()
        pltpu.make_async_copy(s.at[q, pl.ds(4, 2)], extra_rows(x_to, sides, c, mu, mv), sl_l.at[t, c]).start()

    slot_weights = []
    for c in range(3):
        wait_bytes(pw4.at[c, pl.ds(0, 3)], pw_r.at[c])
        wait_bytes(t4[c].at[pl.ds(0, 3)], ag_r.at[0, c])
        both = pw4[c].reshape(256, 128)
        found = dot(selector(c, 0).astype(BF), both.astype(BF), 1, 1)
        pick = jnp.where(found == wanted, 1.0, 0.0)
        p4s[c] = pick.astype(BF)
        slot_weights.append(
            jnp.sum(pick * dot(selector(c, 64), both, 1, 1, precision=HI), axis=1, keepdims=True)
        )
        rows = dot(p4s[c], t4[c][...].reshape(256, WIDTH[c]), 1, 0).astype(BF)
        st[c].reshape(768, WIDTH[c])[...] = rows
        send_slots(st[c], x5, xe, c, 0)
    for c in range(3):
        wait_bytes(g4[c].at[pl.ds(0, 3)], ag_r.at[1, c])
        rows = dot(p4s[c], g4[c][...].reshape(256, WIDTH[c]), 1, 0)
        ss[c].reshape(768, WIDTH[c])[...] = (slot_weights[c] * rows).astype(BF)
        send_slots(ss[c], d5, de, c, 1)

    def moved(v, c):
        if c == 1:
            return (v & 0xC3) | ((v >> 2) & 0x0C) | ((v << 2) & 0x30)
        return ((v & 0x0C) << 4) | ((v & 0xF0) >> 2) | (v & 3)

    def take_slots(s, x_to, sides, t):
        for c in range(3):
            wait_bytes(s[c].at[pl.ds(0, 15)], sl_r.at[t, c])
            wait_bytes(s[c].at[0], sl_l.at[t, c])
        flat = x_to.reshape(768, D)
        for c in (1, 2):
            order = jnp.where(iota((256, 256), 0) == moved(iota((256, 256), 1), c), 1.0, 0.0).astype(BF)
            flat[512:768, FIRST[c] : FIRST[c] + WIDTH[c]] = dot(
                order, sides[c][...].reshape(256, WIDTH[c]), 1, 0
            ).astype(BF)

    wait_bytes(wgu_half, wt_r.at[0])
    take_slots(st, x5, xe, 0)

    def forward(i, carry):
        rows = pl.ds(pl.multiple_of(i * 256, 256), 256)
        token_rows = x5.reshape(768, D)[rows, :]
        pre = dot(token_rows, wgu[...], 1, 0)
        gate, up = pre[:, :FF], pre[:, FF:]
        sig = sigmoid(gate)
        silu = gate * sig
        hid[rows, :] = (silu * up).astype(BF)
        act[rows, :] = silu
        fac[rows, :] = up * sig * (1.0 + gate * (1.0 - sig))
        return carry

    lax.fori_loop(0, 3, forward, 0)

    wait_bytes(wd_half, wt_r.at[1])
    take_slots(ss, d5, de, 1)

    def backward(i, carry):
        rows = pl.ds(pl.multiple_of(i * 256, 256), 256)
        grad_hidden = dot(d5.reshape(768, D)[rows, :], wd[...], 1, 1)
        ggu[rows, :FF] = (grad_hidden * fac[rows, :]).astype(BF)
        ggu[rows, FF:] = (grad_hidden * act[rows, :]).astype(BF)
        g5.reshape(768, D)[rows, :] = dot(ggu[rows, :], wgu[...], 1, 1).astype(BF)
        return carry

    lax.fori_loop(0, 3, backward, 0)

    for c in (1, 2):
        order = jnp.where(moved(iota((256, 256), 0), c) == iota((256, 256), 1), 1.0, 0.0).astype(BF)
        ge[c].reshape(256, WIDTH[c])[...] = dot(
            order, g5.reshape(768, D)[512:768, FIRST[c] : FIRST[c] + WIDTH[c]], 1, 0
        ).astype(BF)

    for c in range(3):
        def back(i, carry, c=c):
            o = jnp.where(i < 6, 10 + i, i - 5)
            u, v, who = plane_peer(c, o)
            to = rr[c].at[plane_me[c]]
            remote(main_rows(g5, c, u, v), to.at[pl.ds(0, 4)], rt_s.at[c], rt_r.at[c], who, d).start()
            remote(extra_rows(g5, ge, c, u, v), to.at[pl.ds(4, 2)], rt_s.at[c], rt_r.at[c], who, d).start()
            return carry

        lax.fori_loop(0, 15, back, 0)
        mu, mv = plane_uv[c]
        to = rr[c].at[plane_me[c]]
        pltpu.make_async_copy(main_rows(g5, c, mu, mv), to.at[pl.ds(0, 4)], rt_l.at[c]).start()
        pltpu.make_async_copy(extra_rows(g5, ge, c, mu, mv), to.at[pl.ds(4, 2)], rt_l.at[c]).start()

    def sums_in(j, carry):
        wide = pl.ds(pl.multiple_of(j * 512, 512), 512)
        grads = dot(x5.reshape(768, D)[:, wide], ggu[...], 0, 0)
        for g in range(4):
            low = logu[pl.ds(j * 4 + g, 1), :]
            grad = grads[g * 128 : (g + 1) * 128]
            value = wgu[pl.ds(j * 512 + g * 128, 128), :].astype(F32)
            at = pl.ds((j % 2) * 4 + g, 1)
            sbi[j // 2, 0, at, :] = jnp.sum(grad * (value + low), axis=0, keepdims=True)
            sbi[j // 2, 1, at, :] = jnp.sum(grad, axis=0, keepdims=True)
        return carry

    lax.fori_loop(0, 4, sums_in, 0)
    sbi_out = sbi.at[other]
    remote(sbi_out, rbi, sm_s.at[0], sm_r.at[0], e, other).start()

    def sums_out(j, carry):
        wide = pl.ds(pl.multiple_of(j * 512, 512), 512)
        grads = dot(hid[...], d5.reshape(768, D)[:, wide], 0, 0)
        low = loo[:, wide]
        total = [[jnp.zeros((1, 512), F32)] * 6, [jnp.zeros((1, 512), F32)] * 6]
        for k, r0, groups in down_blocks():
            grad = grads[k * 256 + r0 : k * 256 + r0 + 32]
            value = wd[k * 256 + r0 : k * 256 + r0 + 32, wide].astype(F32)
            row = iota((32, 512), 0)
            for g, first, last in groups:
                mine = grad
                if len(groups) > 1:
                    mine = jnp.where((row >= first) & (row < last), grad, 0.0)
                total[0][g] = total[0][g] + jnp.sum(mine * (value + low[g][None]), axis=0, keepdims=True)
                total[1][g] = total[1][g] + jnp.sum(mine, axis=0, keepdims=True)
        at = pl.ds(pl.multiple_of((j % 2) * 512, 512), 512)
        for t in range(2):
            for g in range(6):
                sbo[j // 2, t, g : g + 1, at] = total[t][g]
        return carry

    lax.fori_loop(0, 4, sums_out, 0)
    sbo_out = sbo.at[other]
    remote(sbo_out, rbo, sm_s.at[1], sm_r.at[1], e, other).start()

    for c in range(3):
        wait_bytes(rr[c].at[pl.ds(0, 15)], rt_r.at[c])
        wait_bytes(rr[c].at[0], rt_l.at[c])
        sums = dot(p4s[c], rr[c].reshape(768, WIDTH[c])[...], 0, 0).astype(BF)
        part[c][...] = sums.reshape(4, TOK, WIDTH[c])
        for k in (2, 1, 3):
            s, who = line_peer(c, k)
            remote(part[c].at[s], got[c].at[here[c]], pt_s.at[c], pt_r.at[c], who, d).start()

    wait_bytes(rbi, sm_r.at[0])
    share = pl.ds(pl.multiple_of(d * 8, 8), 8)
    upper_sum = (sbi[d, 0] + rbi[0]) / (upgu[share, :] + logu[share, :])
    lower_sum = upper_sum - (sbi[d, 1] + rbi[1])
    for p in range(2):
        for t, total in enumerate((upper_sum, lower_sum)):
            plain = dot(total[:, p * FF : (p + 1) * FF], perm, 1, 1, precision=HI)
            sig = sigmoid(clin[p, t, share, :])
            o_in[0, p, t] = plain * rgin[p, t, share, :] * sig * (1.0 - sig)
    wait_bytes(rbo, sm_r.at[1])
    span = upo[:, half] + loo[:, half]
    upper_out = (sbo[d, 0] + rbo[0])[:6] / span
    lower_out = upper_out - (sbo[d, 1] + rbo[1])[:6]
    for t, total in enumerate((upper_out, lower_out)):
        sig = sigmoid(clout[t, :, half])
        o_out[0, t] = total * rgout[t, :, half] * sig * (1.0 - sig)

    for c in range(3):
        wait_bytes(got[c].at[pl.ds(0, 3)], pt_r.at[c])
        total = part[c][here[c]].astype(F32)
        for k in (1, 2, 3):
            s, _ = line_peer(c, k)
            total = total + got[c][s].astype(F32)
        o_tok[:, cols[c]] = total.astype(BF)

    for c in range(3):
        wait_bytes(pw4.at[c, pl.ds(0, 3)], pw_s.at[c])
        wait_bytes(t4[c].at[pl.ds(0, 3)], ag_s.at[0, c])
        wait_bytes(g4[c].at[pl.ds(0, 3)], ag_s.at[1, c])
        for t, s in enumerate((st, ss)):
            wait_bytes(s[c].at[pl.ds(0, 15)], sl_s.at[t, c])
        wait_bytes(rr[c].at[pl.ds(0, 15)], rt_s.at[c])
        wait_bytes(got[c].at[pl.ds(0, 3)], pt_s.at[c])
    wait_bytes(wgu_half, wt_s.at[0])
    wait_bytes(wd_half, wt_s.at[1])
    wait_bytes(sbi_out, sm_s.at[0])
    wait_bytes(sbo_out, sm_s.at[1])


def body(tokens, grad_out, expert_ids, router_weights, codes_in, codes_out, clip_in, range_in, clip_out, range_out):
    def vm(*shape, t=BF):
        return pltpu.VMEM(shape, t)

    dma = pltpu.SemaphoreType.DMA
    scratch = [vm(TOK, 128, t=F32)]
    scratch += [vm(4, TOK, w) for w in WIDTH] * 2 + [vm(3, 4, TOK, 128, t=F32)]
    scratch += [vm(16, 6, 8, w) for w in WIDTH] * 2
    scratch += [vm(6, 4, 4, 8, D)] * 3
    scratch += [vm(16, 2, 8, w) for w in WIDTH[1:]] * 3
    scratch += [vm(16, 6, 8, w) for w in WIDTH] + [vm(3, 768, 256)]
    scratch += [vm(D, 2 * FF), vm(FF, D), vm(16, 2 * FF, t=F32), vm(16, 2 * FF, t=F32), vm(6, D, t=F32), vm(6, D, t=F32)]
    scratch += [vm(768, FF), vm(768, 2 * FF), vm(768, FF, t=F32), vm(768, FF, t=F32)]
    scratch += [vm(4, TOK, w) for w in WIDTH] * 2
    scratch += [vm(2, 2, 8, 2 * FF, t=F32), vm(2, 2, 8, 1024, t=F32), vm(2, 8, 2 * FF, t=F32), vm(2, 8, 1024, t=F32)]
    scratch += [dma((2, 3)), dma((2, 3)), dma((3,)), dma((3,)), dma((2, 3)), dma((2, 3)), dma((2, 3))]
    scratch += [dma((3,)), dma((3,)), dma((3,)), dma((3,)), dma((3,)), dma((2,)), dma((2,)), dma((2,)), dma((2,))]
    args = (
        tokens, grad_out, expert_ids, router_weights, codes_in[0], codes_out[0],
        clip_in[0], range_in[0], clip_out[0], range_out[0],
    )
    vmem = pl.BlockSpec(memory_space=pltpu.VMEM)
    return tuple(
        pl.pallas_call(
            kernel,
            out_shape=(
                jax.ShapeDtypeStruct((TOK, D), BF),
                jax.ShapeDtypeStruct((1, 2, 2, 8, FF), F32),
                jax.ShapeDtypeStruct((1, 2, 6, 1024), F32),
            ),
            in_specs=[vmem] * len(args),
            out_specs=(vmem,) * 3,
            scratch_shapes=scratch,
            compiler_params=pltpu.CompilerParams(
                collective_id=0, has_side_effects=True, vmem_limit_bytes=62 << 20
            ),
        )(*args)
    )


def solution(mesh):
    return jax.shard_map(
        body,
        mesh=mesh,
        in_specs=(
            P(("expert", "dp"), None),
            P(("expert", "dp"), None),
            P(("expert", "dp"), None),
            P(("expert", "dp"), None),
            P("expert", None, "dp", None),
            P("expert", None, "dp"),
            P("expert", None, None, None, None),
            P("expert", None, None, None, None),
            P("expert", None, None, None),
            P("expert", None, None, None),
        ),
        out_specs=(
            P(("expert", "dp"), None),
            P("expert", None, None, "dp", None),
            P("expert", None, None, "dp"),
        ),
        check_vma=False,
    )
```

```python
import functools

import jax
import jax.numpy as jnp
from jax import lax
from jax.experimental import pallas as pl
from jax.experimental.pallas import tpu as pltpu
from jax.sharding import PartitionSpec as P

MESH = pl.DeviceIdType.MESH
D, FF, TOK = 2048, 768, 64
WIDTH = (640, 640, 768)
FIRST = (0, 640, 1280)
BF, F32, I32 = jnp.bfloat16, jnp.float32, jnp.int32
HI = lax.Precision.HIGHEST


def dot(a, b, da, db, **kw):
    return lax.dot_general(a, b, (((da,), (db,)), ((), ())), preferred_element_type=F32, **kw)


def iota(shape, dim):
    return lax.broadcasted_iota(I32, shape, dim)


def sigmoid(v):
    return 1.0 / (1.0 + jnp.exp(-v))


def down_blocks():
    out = []
    for k in range(3):
        for block in range(8):
            rows = range(block * 32, block * 32 + 32)
            groups = {}
            for r in rows:
                groups.setdefault((3 * r + k) // 128, []).append(r - block * 32)
            out.append((k, block * 32, [(g, min(v), max(v) + 1) for g, v in sorted(groups.items())]))
    return out


def split3(v):
    high = v.astype(BF)
    rest = v - high.astype(F32)
    mid = rest.astype(BF)
    low = (rest - mid.astype(F32)).astype(BF)
    return jnp.concatenate([high, mid, low], axis=0)


def join3(v):
    n = v.shape[0] // 3
    return (v[2 * n :] + v[n : 2 * n]) + v[:n]


def nibble_order():
    return jnp.where(
        iota((FF, FF), 0) == 3 * (iota((FF, FF), 1) & 255) + (iota((FF, FF), 1) >> 8), 1.0, 0.0
    ).astype(BF)


def kernel(
    tok, go, ids, rw, cin, cout, clin, rgin, clout, rgout,
    o_tok, o_in, o_out,
    posw, t4a, t4b, t4c, g4a, g4b, g4c, pw4,
    sma, smb, smc, dma_, dmb, dmc, sxa, sxb, sxc, dxa, dxb, dxc,
    x5, d5, g5, xeb, xec, deb, dec, geb, gec,
    rma, rmb, rmc, rxa, rxb, rxc, p4s,
    wgu, wd, upgu, logu, upo, loo, cinv, coutv,
    hid, ggu, fac, act, qa, qb, qc, ha, hb, hc,
    sbi, sbo, rbi, rbo,
    in_l, ag_s, ag_r, pw_s, pw_r, sl_s, sl_r, sl_l, rt_s, rt_r, rt_l, pt_s, pt_r, wt_s, wt_r, sm_s, sm_r,
):
    e, d = lax.axis_index("expert"), lax.axis_index("dp")
    z, y, x = e // 16, (e // 4) % 4, e % 4
    here = (x, y, z)
    t4, g4 = (t4a, t4b, t4c), (g4a, g4b, g4c)
    s_main, s_tail = ((sma, smb, smc), (dma_, dmb, dmc)), ((sxa, sxb, sxc), (dxa, dxb, dxc))
    xe, de, ge = (None, xeb, xec), (None, deb, dec), (None, geb, gec)
    r_main, r_tail = (rma, rmb, rmc), (rxa, rxb, rxc)
    part, got = (qa, qb, qc), (ha, hb, hc)
    cols = [pl.ds(FIRST[c], WIDTH[c]) for c in range(3)]

    def expert_at(zz, yy, xx):
        return zz * 16 + yy * 4 + xx

    def line_peer(c, k):
        s = (here[c] + k) % 4
        return s, (expert_at(z, y, s), expert_at(z, s, x), expert_at(s, y, x))[c]

    def plane_peer(c, o):
        a, b = o // 4, o % 4
        u, v = ((z, y), (z, x), (y, x))[c]
        u, v = (u + a) % 4, (v + b) % 4
        return u, v, (expert_at(u, v, x), expert_at(u, y, v), expert_at(z, u, v))[c]

    def main_rows(ref, c, u, v):
        if c == 0:
            return ref.at[u, v, :, :, cols[c]]
        if c == 1:
            return ref.at[u, :, v, :, cols[c]]
        return ref.at[pl.ds(0, 4), u, v, :, cols[c]]

    def tail_rows(ref, sides, c, u, v):
        if c == 0:
            return ref.at[4 + u // 2, (u % 2) * 2 + v // 2, pl.ds((v % 2) * 2, 2), :, cols[c]]
        return sides[c].at[u * 4 + v]

    def remote(src, dst, s, r, who, core):
        return pltpu.make_async_remote_copy(
            src_ref=src, dst_ref=dst, send_sem=s, recv_sem=r, device_id=(who, core), device_id_type=MESH
        )

    def wait_bytes(ref, sem):
        pltpu.make_async_copy(ref, ref, sem).wait()

    plane_me = (z * 4 + y, z * 4 + x, y * 4 + x)
    plane_uv = ((z, y), (z, x), (y, x))

    barrier = pltpu.get_barrier_semaphore()
    greeted = [(a, b, c) for a in range(4) for b in range(4) for c in range(4) if 0 in (a, b, c) and (a, b, c) != (0, 0, 0)]
    for a, b, c in greeted:
        who = expert_at((z + a) % 4, (y + b) % 4, (x + c) % 4)
        pl.semaphore_signal(barrier, inc=1, device_id=(who, d), device_id_type=MESH)
    pl.semaphore_signal(barrier, inc=1, device_id=(e, 1 - d), device_id_type=MESH)

    for c in range(3):
        pltpu.make_async_copy(tok.at[:, cols[c]], t4[c].at[here[c]], in_l.at[c]).start()
    codes_in = pltpu.make_async_copy(cin, cinv, in_l.at[6])
    codes_out = pltpu.make_async_copy(cout, coutv, in_l.at[7])
    codes_in.start()
    codes_out.start()
    for c in range(3):
        pltpu.make_async_copy(go.at[:, cols[c]], g4[c].at[here[c]], in_l.at[3 + c]).start()

    row = iota((128, TOK), 0)
    chosen = jnp.zeros((128, TOK), F32)
    weight = jnp.zeros((128, TOK), F32)
    for k in range(8):
        ident = ids[k : k + 1, :]
        chosen = chosen + jnp.where(row == ident, 1.0, 0.0)
        weight = weight + jnp.where(row == ident + 64, rw[k : k + 1, :], 0.0)
    earlier = jnp.where(iota((TOK, TOK), 0) < iota((TOK, TOK), 1), 1.0, 0.0).astype(BF)
    before = dot(chosen.astype(BF), earlier, 1, 0)
    rank = jnp.where(chosen > 0.5, before, jnp.where(row < 64, -64.0, 0.0)) + weight
    posw[...] = rank.T
    for c in range(3):
        pw4[c, here[c]] = posw[...]

    ends = [sigmoid(clin[p, t]) * rgin[p, t] for p in range(2) for t in range(2)]
    ends = join3(dot(split3(jnp.concatenate(ends, axis=0)), nibble_order(), 1, 0))
    for p in range(2):
        upgu[:, p * FF : (p + 1) * FF] = ends[p * 32 : p * 32 + 16]
        logu[:, p * FF : (p + 1) * FF] = ends[p * 32 + 16 : p * 32 + 32]
    for g in range(6):
        end = sigmoid(clout[g]) * rgout[g]
        upo[g : g + 1, :] = end[0:1]
        loo[g : g + 1, :] = end[1:2]

    codes_in.wait()
    codes_out.wait()

    def dequant_in(g, carry):
        up = upgu[pl.ds(d * 8 + g, 1), :]
        lo = logu[pl.ds(d * 8 + g, 1), :]
        step = (up + lo) / 15.0
        for p in range(2):
            words = cinv[p, pl.ds(g * 128, 128), :]
            for k in range(3):
                c0 = p * FF + k * 256
                code = ((words >> (4 * k)) & 15).astype(F32)
                wgu[pl.ds(d * 1024 + g * 128, 128), c0 : c0 + 256] = (
                    code * step[:, c0 : c0 + 256] - lo[:, c0 : c0 + 256]
                ).astype(BF)
        return carry

    lax.fori_loop(0, 8, dequant_in, 0)
    half = pl.ds(pl.multiple_of(d * 1024, 1024), 1024)
    up_half, lo_half = upo[:, half], loo[:, half]
    step_half = (up_half + lo_half) / 15.0
    for k, r0, groups in down_blocks():
        code = ((coutv[r0 : r0 + 32, :] >> (4 * k)) & 15).astype(F32)
        unit = iota((32, 1024), 0)
        scale, shift = step_half[groups[0][0]][None], lo_half[groups[0][0]][None]
        for g, first, _ in groups[1:]:
            scale = jnp.where(unit >= first, step_half[g][None], scale)
            shift = jnp.where(unit >= first, lo_half[g][None], shift)
        wd[k * 256 + r0 : k * 256 + r0 + 32, half] = (code * scale - shift).astype(BF)

    for c in range(3):
        wait_bytes(t4[c].at[here[c]], in_l.at[c])
        wait_bytes(g4[c].at[here[c]], in_l.at[3 + c])
    pl.semaphore_wait(barrier, len(greeted) + 1)

    for k in (2, 1, 3):
        for c in range(3):
            _, who = line_peer(c, k)
            remote(posw, pw4.at[c, here[c]], pw_s.at[c], pw_r.at[c], who, d).start()
    for k in (2, 1, 3):
        for c in range(3):
            _, who = line_peer(c, k)
            mine = t4[c].at[here[c]]
            remote(mine, mine, ag_s.at[0, c], ag_r.at[0, c], who, d).start()
    for k in (2, 1, 3):
        for c in range(3):
            _, who = line_peer(c, k)
            mine = g4[c].at[here[c]]
            remote(mine, mine, ag_s.at[1, c], ag_r.at[1, c], who, d).start()

    other = 1 - d
    wgu_half = wgu.at[pl.ds(pl.multiple_of(d * 1024, 1024), 1024), :]
    wd_half = wd.at[:, half]
    remote(wgu_half, wgu_half, wt_s.at[0], wt_r.at[0], e, other).start()
    remote(wd_half, wd_half, wt_s.at[1], wt_r.at[1], e, other).start()

    def selector(c, first):
        def rows(n):
            q = iota((16, n, 128), 0)
            u, v = q >> 2, q & 3
            target = (u * 16 + v * 4 + x, u * 16 + y * 4 + v, z * 16 + u * 4 + v)[c]
            return jnp.where(iota((16, n, 128), 2) == target + first, 1.0, 0.0).reshape(16 * n, 128)

        return jnp.concatenate([rows(32), rows(16)], axis=0).astype(BF)

    r = iota((16, 32, 256), 1)
    want_main = (r >> 3) * 16 + (r & 7) - 16 * (iota((16, 32, 256), 2) >> 6)
    r = iota((16, 16, 256), 1)
    want_tail = (r >> 2) * 16 + 8 + (r & 3) - 16 * (iota((16, 16, 256), 2) >> 6)
    wanted = jnp.concatenate([want_main.reshape(512, 256), want_tail.reshape(256, 256)], axis=0).astype(F32)

    def spread(c, t, src, to):
        def one(i, carry):
            o = jnp.where(i < 6, 10 + i, i - 5)
            u, v, who = plane_peer(c, o)
            remote(src.at[u * 4 + v], to, sl_s.at[t, c], sl_r.at[t, c], who, d).start()
            return carry

        lax.fori_loop(0, 15, one, 0)
        pltpu.make_async_copy(src.at[plane_me[c]], to, sl_l.at[t, c]).start()

    for c in range(3):
        wait_bytes(pw4.at[c, pl.ds(0, 3)], pw_r.at[c])
        found = dot(selector(c, 0), pw4[c].reshape(256, 128).astype(BF), 1, 1)
        p4s[c] = jnp.where(found == wanted, 1.0, 0.0).astype(BF)
    for c in range(3):
        wait_bytes(t4[c].at[pl.ds(0, 3)], ag_r.at[0, c])
        rows = dot(p4s[c, :512], t4[c][...].reshape(256, WIDTH[c]), 1, 0).astype(BF)
        s_main[0][c].reshape(512, WIDTH[c])[...] = rows
        spread(c, 0, s_main[0][c], main_rows(x5, c, *plane_uv[c]))
    slot_weights = []
    for c in range(3):
        parts = split3(pw4[c].reshape(256, 128))
        named = dot(selector(c, 64), parts, 1, 1)
        named = (named[:, 512:] + named[:, 256:512]) + named[:, :256]
        slot_weights.append(jnp.sum(p4s[c].astype(F32) * named, axis=1, keepdims=True))
    for c in range(3):
        wait_bytes(g4[c].at[pl.ds(0, 3)], ag_r.at[1, c])
        rows = dot(p4s[c, :512], g4[c][...].reshape(256, WIDTH[c]), 1, 0)
        s_main[1][c].reshape(512, WIDTH[c])[...] = (slot_weights[c][:512] * rows).astype(BF)
        spread(c, 1, s_main[1][c], main_rows(d5, c, *plane_uv[c]))
    for c in range(3):
        rows = dot(p4s[c, 512:], t4[c][...].reshape(256, WIDTH[c]), 1, 0).astype(BF)
        s_tail[0][c].reshape(256, WIDTH[c])[...] = rows
        spread(c, 2, s_tail[0][c], tail_rows(x5, xe, c, *plane_uv[c]))
    for c in range(3):
        rows = dot(p4s[c, 512:], g4[c][...].reshape(256, WIDTH[c]), 1, 0)
        s_tail[1][c].reshape(256, WIDTH[c])[...] = (slot_weights[c][512:] * rows).astype(BF)
        spread(c, 3, s_tail[1][c], tail_rows(d5, de, c, *plane_uv[c]))

    def moved(v, c):
        if c == 1:
            return (v & 0xC3) | ((v >> 2) & 0x0C) | ((v << 2) & 0x30)
        return ((v & 0x0C) << 4) | ((v & 0xF0) >> 2) | (v & 3)

    def arrived(t, src):
        for c in range(3):
            wait_bytes(src[c].at[pl.ds(0, 15)], sl_r.at[t, c])
            wait_bytes(src[c].at[0], sl_l.at[t, c])

    def order_tail(to, sides):
        for c in (1, 2):
            order = jnp.where(iota((256, 256), 0) == moved(iota((256, 256), 1), c), 1.0, 0.0).astype(BF)
            to.reshape(768, D)[512:768, FIRST[c] : FIRST[c] + WIDTH[c]] = dot(
                order, sides[c][...].reshape(256, WIDTH[c]), 1, 0
            ).astype(BF)

    def forward(i, carry):
        rows = pl.ds(pl.multiple_of(i * 256, 256), 256)
        token_rows = x5.reshape(768, D)[rows, :]
        pre = dot(token_rows, wgu[...], 1, 0)
        gate, up = pre[:, :FF], pre[:, FF:]
        sig = sigmoid(gate)
        silu = gate * sig
        hid[rows, :] = (silu * up).astype(BF)
        act[rows, :] = silu
        fac[rows, :] = up * sig * (1.0 + gate * (1.0 - sig))
        return carry

    def backward(i, carry):
        rows = pl.ds(pl.multiple_of(i * 256, 256), 256)
        grad_hidden = dot(d5.reshape(768, D)[rows, :], wd[...], 1, 1)
        ggu[rows, :FF] = (grad_hidden * fac[rows, :]).astype(BF)
        ggu[rows, FF:] = (grad_hidden * act[rows, :]).astype(BF)
        g5.reshape(768, D)[rows, :] = dot(ggu[rows, :], wgu[...], 1, 1).astype(BF)
        return carry

    def give_back(t, dst, rows_of):
        for c in range(3):
            to = dst[c].at[plane_me[c]]

            def one(i, carry, c=c, to=to):
                o = jnp.where(i < 6, 10 + i, i - 5)
                u, v, who = plane_peer(c, o)
                remote(rows_of(c, u, v), to, rt_s.at[t, c], rt_r.at[t, c], who, d).start()
                return carry

            lax.fori_loop(0, 15, one, 0)
            pltpu.make_async_copy(rows_of(c, *plane_uv[c]), to, rt_l.at[t, c]).start()

    wait_bytes(wgu_half, wt_r.at[0])
    wait_bytes(wd_half, wt_r.at[1])
    arrived(0, s_main[0])
    lax.fori_loop(0, 2, forward, 0)
    arrived(1, s_main[1])
    lax.fori_loop(0, 2, backward, 0)
    give_back(0, r_main, lambda c, u, v: main_rows(g5, c, u, v))

    arrived(2, s_tail[0])
    order_tail(x5, xe)
    lax.fori_loop(2, 3, forward, 0)
    arrived(3, s_tail[1])
    order_tail(d5, de)
    lax.fori_loop(2, 3, backward, 0)
    for c in (1, 2):
        order = jnp.where(moved(iota((256, 256), 0), c) == iota((256, 256), 1), 1.0, 0.0).astype(BF)
        ge[c].reshape(256, WIDTH[c])[...] = dot(
            order, g5.reshape(768, D)[512:768, FIRST[c] : FIRST[c] + WIDTH[c]], 1, 0
        ).astype(BF)
    give_back(1, r_tail, lambda c, u, v: tail_rows(g5, ge, c, u, v))

    def sums_in(j, carry):
        wide = pl.ds(pl.multiple_of(j * 512, 512), 512)
        grads = dot(x5.reshape(768, D)[:, wide], ggu[...], 0, 0)
        for g in range(4):
            low = logu[pl.ds(j * 4 + g, 1), :]
            grad = grads[g * 128 : (g + 1) * 128]
            value = wgu[pl.ds(j * 512 + g * 128, 128), :].astype(F32)
            at = pl.ds((j % 2) * 4 + g, 1)
            sbi[j // 2, 0, at, :] = jnp.sum(grad * (value + low), axis=0, keepdims=True)
            sbi[j // 2, 1, at, :] = jnp.sum(grad, axis=0, keepdims=True)
        return carry

    lax.fori_loop(0, 4, sums_in, 0)
    sbi_out = sbi.at[other]
    remote(sbi_out, rbi, sm_s.at[0], sm_r.at[0], e, other).start()

    def sums_out(j, carry):
        wide = pl.ds(pl.multiple_of(j * 512, 512), 512)
        grads = dot(hid[...], d5.reshape(768, D)[:, wide], 0, 0)
        low = loo[:, wide]
        total = [[jnp.zeros((1, 512), F32)] * 6, [jnp.zeros((1, 512), F32)] * 6]
        for k, r0, groups in down_blocks():
            grad = grads[k * 256 + r0 : k * 256 + r0 + 32]
            value = wd[k * 256 + r0 : k * 256 + r0 + 32, wide].astype(F32)
            unit = iota((32, 512), 0)
            for g, first, last in groups:
                mine = grad
                if len(groups) > 1:
                    mine = jnp.where((unit >= first) & (unit < last), grad, 0.0)
                total[0][g] = total[0][g] + jnp.sum(mine * (value + low[g][None]), axis=0, keepdims=True)
                total[1][g] = total[1][g] + jnp.sum(mine, axis=0, keepdims=True)
        at = pl.ds(pl.multiple_of((j % 2) * 512, 512), 512)
        for t in range(2):
            for g in range(6):
                sbo[j // 2, t, g : g + 1, at] = total[t][g]
        return carry

    lax.fori_loop(0, 4, sums_out, 0)
    sbo_out = sbo.at[other]
    remote(sbo_out, rbo, sm_s.at[1], sm_r.at[1], e, other).start()

    wait_bytes(rbi, sm_r.at[0])
    share = pl.ds(pl.multiple_of(d * 8, 8), 8)
    upper_sum = (sbi[d, 0] + rbi[0]) / (upgu[share, :] + logu[share, :])
    lower_sum = upper_sum - (sbi[d, 1] + rbi[1])
    totals = [total[:, p * FF : (p + 1) * FF] for p in range(2) for total in (upper_sum, lower_sum)]
    plain = join3(dot(split3(jnp.concatenate(totals, axis=0)), nibble_order(), 1, 1))
    for p in range(2):
        for t in range(2):
            sig = sigmoid(clin[p, t, share, :])
            total = plain[(p * 2 + t) * 8 : (p * 2 + t) * 8 + 8]
            o_in[0, p, t] = total * rgin[p, t, share, :] * sig * (1.0 - sig)
    wait_bytes(rbo, sm_r.at[1])
    span = upo[:, half] + loo[:, half]
    upper_out = (sbo[d, 0] + rbo[0])[:6] / span
    lower_out = upper_out - (sbo[d, 1] + rbo[1])[:6]
    for g in range(6):
        sig = sigmoid(clout[g, :, half])
        total = jnp.concatenate([upper_out[g : g + 1], lower_out[g : g + 1]], axis=0)
        o_out[g] = total * rgout[g, :, half] * sig * (1.0 - sig)

    sums = []
    for c in range(3):
        wait_bytes(s_main[0][c].at[pl.ds(0, 15)], rt_r.at[0, c])
        wait_bytes(s_main[0][c].at[0], rt_l.at[0, c])
        sums.append(dot(p4s[c, :512], r_main[c].reshape(512, WIDTH[c])[...], 0, 0))
    for c in range(3):
        wait_bytes(s_tail[0][c].at[pl.ds(0, 15)], rt_r.at[1, c])
        wait_bytes(s_tail[0][c].at[0], rt_l.at[1, c])
        total = sums[c] + dot(p4s[c, 512:], r_tail[c].reshape(256, WIDTH[c])[...], 0, 0)
        part[c][...] = total.astype(BF).reshape(4, TOK, WIDTH[c])
        for k in (2, 1, 3):
            s, who = line_peer(c, k)
            remote(part[c].at[s], got[c].at[here[c]], pt_s.at[c], pt_r.at[c], who, d).start()
    for c in range(3):
        wait_bytes(got[c].at[pl.ds(0, 3)], pt_r.at[c])
        total = part[c][here[c]].astype(F32)
        for k in (1, 2, 3):
            s, _ = line_peer(c, k)
            total = total + got[c][s].astype(F32)
        o_tok[:, cols[c]] = total.astype(BF)

    for c in range(3):
        wait_bytes(pw4.at[c, pl.ds(0, 3)], pw_s.at[c])
        wait_bytes(t4[c].at[pl.ds(0, 3)], ag_s.at[0, c])
        wait_bytes(g4[c].at[pl.ds(0, 3)], ag_s.at[1, c])
        for t in range(2):
            wait_bytes(s_main[t][c].at[pl.ds(0, 15)], sl_s.at[t, c])
            wait_bytes(s_tail[t][c].at[pl.ds(0, 15)], sl_s.at[2 + t, c])
        wait_bytes(s_main[0][c].at[pl.ds(0, 15)], rt_s.at[0, c])
        wait_bytes(s_tail[0][c].at[pl.ds(0, 15)], rt_s.at[1, c])
        wait_bytes(got[c].at[pl.ds(0, 3)], pt_s.at[c])
    wait_bytes(wgu_half, wt_s.at[0])
    wait_bytes(wd_half, wt_s.at[1])
    wait_bytes(sbi_out, sm_s.at[0])
    wait_bytes(sbo_out, sm_s.at[1])


def hand_out(a, b, c, to_a, to_b, to_c):
    to_a[...] = a[...]
    to_b[...] = b[...]
    to_c[...] = c[...]


def body(tokens, grad_out, expert_ids, router_weights, codes_in, codes_out, clip_in, range_in, clip_out, range_out):
    def vm(*shape, t=BF):
        return pltpu.VMEM(shape, t)

    dma = pltpu.SemaphoreType.DMA
    scratch = [vm(TOK, 128, t=F32)]
    scratch += [vm(4, TOK, w) for w in WIDTH] * 2 + [vm(3, 4, TOK, 128, t=F32)]
    scratch += [vm(16, 4, 8, w) for w in WIDTH] * 2 + [vm(16, 2, 8, w) for w in WIDTH] * 2
    scratch += [vm(6, 4, 4, 8, D)] * 3
    scratch += [vm(16, 2, 8, w) for w in WIDTH[1:]] * 3
    scratch += [vm(16, 4, 8, w) for w in WIDTH] + [vm(16, 2, 8, w) for w in WIDTH] + [vm(3, 768, 256)]
    scratch += [vm(D, 2 * FF), vm(FF, D), vm(16, 2 * FF, t=F32), vm(16, 2 * FF, t=F32), vm(6, D, t=F32), vm(6, D, t=F32)]
    scratch += [vm(2, 1024, 256, t=I32), vm(256, 1024, t=I32)]
    scratch += [vm(768, FF), vm(768, 2 * FF), vm(768, FF, t=F32), vm(768, FF, t=F32)]
    scratch += [vm(4, TOK, w) for w in WIDTH] * 2
    scratch += [vm(2, 2, 8, 2 * FF, t=F32), vm(2, 2, 8, 1024, t=F32), vm(2, 8, 2 * FF, t=F32), vm(2, 8, 1024, t=F32)]
    scratch += [dma((8,)), dma((2, 3)), dma((2, 3)), dma((3,)), dma((3,)), dma((4, 3)), dma((4, 3)), dma((4, 3))]
    scratch += [dma((2, 3)), dma((2, 3)), dma((2, 3)), dma((3,)), dma((3,)), dma((2,)), dma((2,)), dma((2,)), dma((2,))]
    args = (
        tokens, grad_out, expert_ids.T, router_weights.T, codes_in[0], codes_out[0],
        clip_in[0], range_in[0], clip_out[0].transpose(1, 0, 2), range_out[0].transpose(1, 0, 2),
    )
    vmem, anywhere = pl.BlockSpec(memory_space=pltpu.VMEM), pl.BlockSpec(memory_space=pl.ANY)
    results = (
        jax.ShapeDtypeStruct((TOK, D), BF),
        jax.ShapeDtypeStruct((1, 2, 2, 8, FF), F32),
        jax.ShapeDtypeStruct((6, 2, 1024), F32),
    )
    found = pl.pallas_call(
        kernel,
        out_shape=results,
        in_specs=[anywhere, anywhere, vmem, vmem, anywhere, anywhere, vmem, vmem, vmem, vmem],
        out_specs=(vmem,) * 3,
        scratch_shapes=scratch,
        compiler_params=pltpu.CompilerParams(collective_id=0, has_side_effects=True, vmem_limit_bytes=62 << 20),
    )(*args)
    grad_tokens, grad_in, grad_out_clip = pl.pallas_call(
        hand_out, out_shape=results, in_specs=[vmem] * 3, out_specs=(vmem,) * 3
    )(*found)
    return grad_tokens, grad_in, grad_out_clip.transpose(1, 0, 2)[None]


def solution(mesh):
    return jax.shard_map(
        body,
        mesh=mesh,
        in_specs=(
            P(("expert", "dp"), None),
            P(("expert", "dp"), None),
            P(("expert", "dp"), None),
            P(("expert", "dp"), None),
            P("expert", None, "dp", None),
            P("expert", None, "dp"),
            P("expert", None, None, None, None),
            P("expert", None, None, None, None),
            P("expert", None, None, None),
            P("expert", None, None, None),
        ),
        out_specs=(
            P(("expert", "dp"), None),
            P("expert", None, None, "dp", None),
            P("expert", None, None, "dp"),
        ),
        check_vma=False,
    )
```

```python
import functools

import jax
import jax.numpy as jnp
from jax import lax
from jax.experimental import pallas as pl
from jax.experimental.pallas import tpu as pltpu
from jax.sharding import PartitionSpec as P

MESH = pl.DeviceIdType.MESH
D, FF, TOK = 2048, 768, 64
WIDTH = ((640, 640, 768), (640, 768, 640), (768, 640, 640))
FIRST = ((0, 640, 1280), (0, 640, 1408), (0, 768, 1408))
BF, F32, I32 = jnp.bfloat16, jnp.float32, jnp.int32
HI = lax.Precision.HIGHEST


def dot(a, b, da, db, **kw):
    return lax.dot_general(a, b, (((da,), (db,)), ((), ())), preferred_element_type=F32, **kw)


def iota(shape, dim):
    return lax.broadcasted_iota(I32, shape, dim)


def sigmoid(v):
    return 1.0 / (1.0 + jnp.exp(-v))


def down_blocks():
    out = []
    for k in range(3):
        for block in range(8):
            rows = range(block * 32, block * 32 + 32)
            groups = {}
            for r in rows:
                groups.setdefault((3 * r + k) // 128, []).append(r - block * 32)
            out.append((k, block * 32, [(g, min(v), max(v) + 1) for g, v in sorted(groups.items())]))
    return out


def split3(v):
    high = v.astype(BF)
    rest = v - high.astype(F32)
    mid = rest.astype(BF)
    low = (rest - mid.astype(F32)).astype(BF)
    return jnp.concatenate([high, mid, low], axis=0)


def join3(v):
    n = v.shape[0] // 3
    return (v[2 * n :] + v[n : 2 * n]) + v[:n]


def nibble_order():
    return jnp.where(
        iota((FF, FF), 0) == 3 * (iota((FF, FF), 1) & 255) + (iota((FF, FF), 1) >> 8), 1.0, 0.0
    ).astype(BF)


def kernel(
    tok, go, ids, rw, cin, cout, clin, rgin, clout, rgout,
    o_tok, o_in, o_out,
    tab, t4a, t4b, t4c, g4a, g4b, g4c, pw4,
    sma, smb, smc, dma_, dmb, dmc, sxa, sxb, sxc, dxa, dxb, dxc,
    x5, d5, g5, xeb, xec, deb, dec, geb, gec,
    rma, rmb, rmc, rxa, rxb, rxc, p4s,
    wgu, wd, upgu, logu, upo, loo, cinv, coutv, idv, rwv, clinv, rginv, cloutv, rgoutv,
    hid, ggu, fac, act, qa, qb, qc, ha, hb, hc,
    sbi, sbo, rbi, rbo,
    in_l, ag_s, ag_r, pw_s, pw_r, sl_s, sl_r, sl_l, rt_s, rt_r, rt_l, pt_s, pt_r, wt_s, wt_r, sm_s, sm_r,
):
    e, d = lax.axis_index("expert"), lax.axis_index("dp")
    z, y, x = e // 16, (e // 4) % 4, e % 4
    here = (x, y, z)
    t4, g4 = (t4a, t4b, t4c), (g4a, g4b, g4c)
    s_main, s_tail = ((sma, smb, smc), (dma_, dmb, dmc)), ((sxa, sxb, sxc), (dxa, dxb, dxc))
    xe, de, ge = (None, xeb, xec), (None, deb, dec), (None, geb, gec)
    r_main, r_tail = (rma, rmb, rmc), (rxa, rxb, rxc)
    part, got = (qa, qb, qc), (ha, hb, hc)
    cols = [[pl.ds(FIRST[t][c], WIDTH[t][c]) for c in range(3)] for t in range(3)]

    def expert_at(zz, yy, xx):
        return zz * 16 + yy * 4 + xx

    def line_peer(c, k):
        s = (here[c] + k) % 4
        return s, (expert_at(z, y, s), expert_at(z, s, x), expert_at(s, y, x))[c]

    def plane_peer(c, o):
        a, b = o // 4, o % 4
        u, v = ((z, y), (z, x), (y, x))[c]
        u, v = (u + a) % 4, (v + b) % 4
        return u, v, (expert_at(u, v, x), expert_at(u, y, v), expert_at(z, u, v))[c]

    def nearest(i):
        return jnp.where(i < 7, 0x8DF134C >> (4 * jnp.minimum(i, 6)), 0x6A9BE257 >> (4 * jnp.maximum(i - 7, 0))) & 15

    def main_rows(ref, t, c, u, v):
        if c == 0:
            return ref.at[u, v, :, :, cols[t][c]]
        if c == 1:
            return ref.at[u, :, v, :, cols[t][c]]
        return ref.at[pl.ds(0, 4), u, v, :, cols[t][c]]

    def tail_rows(ref, sides, t, c, u, v):
        if c == 0:
            return ref.at[4 + u // 2, (u % 2) * 2 + v // 2, pl.ds((v % 2) * 2, 2), :, cols[t][c]]
        return sides[c].at[u * 4 + v]

    def remote(src, dst, s, r, who, core):
        return pltpu.make_async_remote_copy(
            src_ref=src, dst_ref=dst, send_sem=s, recv_sem=r, device_id=(who, core), device_id_type=MESH
        )

    def wait_bytes(ref, sem):
        pltpu.make_async_copy(ref, ref, sem).wait()

    plane_me = (z * 4 + y, z * 4 + x, y * 4 + x)
    plane_uv = ((z, y), (z, x), (y, x))

    barrier = pltpu.get_barrier_semaphore()
    for c in range(3):
        for k in (2, 1, 3):
            pl.semaphore_signal(barrier, inc=1, device_id=(line_peer(c, k)[1], d), device_id_type=MESH)
    pl.semaphore_signal(barrier, inc=1, device_id=(e, 1 - d), device_id_type=MESH)

    small = [(ids, idv), (rw, rwv), (clin, clinv), (rgin, rginv), (clout, cloutv), (rgout, rgoutv), (cin, cinv), (cout, coutv)]
    loads = [pltpu.make_async_copy(src, dst, in_l.at[6 + i]) for i, (src, dst) in enumerate(small)]
    loads[0].start()
    loads[1].start()
    for c in range(3):
        pltpu.make_async_copy(tok.at[:, cols[0][c]], t4[c].at[here[c]], in_l.at[c]).start()
    for c in range(3):
        pltpu.make_async_copy(go.at[:, cols[1][c]], g4[c].at[here[c]], in_l.at[3 + c]).start()
    for load in loads[2:]:
        load.start()
    loads[0].wait()
    loads[1].wait()

    row = iota((128, TOK), 0)
    chosen = jnp.zeros((128, TOK), F32)
    weight = jnp.zeros((128, TOK), F32)
    for k in range(8):
        ident = idv[k : k + 1, :]
        chosen = chosen + jnp.where(row == ident, 1.0, 0.0)
        weight = weight + jnp.where(row == ident + 64, rwv[k : k + 1, :], 0.0)
    earlier = jnp.where(iota((TOK, TOK), 0) < iota((TOK, TOK), 1), 1.0, 0.0).astype(BF)
    before = dot(chosen.astype(BF), earlier, 1, 0)
    rank = jnp.where(chosen > 0.5, before, jnp.where(row < 64, -64.0, 0.0))
    table = rank + weight
    high = table.astype(BF).astype(F32)
    left = table - high
    mid = left.astype(BF).astype(F32)
    low = left - mid
    table = jnp.concatenate([high, jnp.concatenate([low[64:], mid[64:]], axis=0)], axis=1).astype(BF)
    plans = []
    for c in range(3):
        s, i = iota((4, 32, 128), 0), iota((4, 32, 128), 1)
        u, v = (i >> 2) & 3, i & 3
        named = (expert_at(u, v, s), expert_at(u, s, v), expert_at(s, u, v))[c] + (i >> 4) * 64
        plans.append(jnp.where(iota((4, 32, 128), 2) == named, 1.0, 0.0).reshape(128, 128))
    plans = jnp.concatenate(plans, axis=0).astype(BF)
    tab.reshape(384, 128)[...] = dot(plans, table, 1, 0).astype(BF)
    for c in range(3):
        pw4[c, here[c]] = tab[c * 4 + here[c]]

    for c in range(3):
        wait_bytes(t4[c].at[here[c]], in_l.at[c])
        wait_bytes(g4[c].at[here[c]], in_l.at[3 + c])
    pl.semaphore_wait(barrier, 10)

    for k in (2, 1, 3):
        for c in range(3):
            at, who = line_peer(c, k)
            remote(tab.at[c * 4 + at], pw4.at[c, here[c]], pw_s.at[c], pw_r.at[c], who, d).start()
    for t, q4 in enumerate((t4, g4)):
        for k in (2, 1, 3):
            for c in range(3):
                _, who = line_peer(c, k)
                mine = q4[c].at[here[c]]
                remote(mine, mine, ag_s.at[t, c], ag_r.at[t, c], who, d).start()

    for load in loads[2:]:
        load.wait()
    ends = [sigmoid(clinv[p, t]) * rginv[p, t] for p in range(2) for t in range(2)]
    ends = join3(dot(split3(jnp.concatenate(ends, axis=0)), nibble_order(), 1, 0))
    for p in range(2):
        upgu[:, p * FF : (p + 1) * FF] = ends[p * 32 : p * 32 + 16]
        logu[:, p * FF : (p + 1) * FF] = ends[p * 32 + 16 : p * 32 + 32]
    for g in range(6):
        end = sigmoid(cloutv[g]) * rgoutv[g]
        upo[g : g + 1, :] = end[0:1]
        loo[g : g + 1, :] = end[1:2]

    def dequant_in(g, carry):
        up = upgu[pl.ds(d * 8 + g, 1), :]
        lo = logu[pl.ds(d * 8 + g, 1), :]
        step = (up + lo) / 15.0
        for p in range(2):
            words = cinv[p, pl.ds(g * 128, 128), :]
            for k in range(3):
                c0 = p * FF + k * 256
                code = ((words >> (4 * k)) & 15).astype(F32)
                wgu[pl.ds(d * 1024 + g * 128, 128), c0 : c0 + 256] = (
                    code * step[:, c0 : c0 + 256] - lo[:, c0 : c0 + 256]
                ).astype(BF)
        return carry

    lax.fori_loop(0, 8, dequant_in, 0)
    half = pl.ds(pl.multiple_of(d * 1024, 1024), 1024)
    up_half, lo_half = upo[:, half], loo[:, half]
    step_half = (up_half + lo_half) / 15.0
    for k, r0, groups in down_blocks():
        code = ((coutv[r0 : r0 + 32, :] >> (4 * k)) & 15).astype(F32)
        unit = iota((32, 1024), 0)
        scale, shift = step_half[groups[0][0]][None], lo_half[groups[0][0]][None]
        for g, first, _ in groups[1:]:
            scale = jnp.where(unit >= first, step_half[g][None], scale)
            shift = jnp.where(unit >= first, lo_half[g][None], shift)
        wd[k * 256 + r0 : k * 256 + r0 + 32, half] = (code * scale - shift).astype(BF)

    other = 1 - d
    wgu_half = wgu.at[pl.ds(pl.multiple_of(d * 1024, 1024), 1024), :]
    wd_half = wd.at[:, half]
    remote(wgu_half, wgu_half, wt_s.at[0], wt_r.at[0], e, other).start()
    remote(wd_half, wd_half, wt_s.at[1], wt_r.at[1], e, other).start()

    def selector(first):
        def rows(n):
            hit = iota((16, n, 32), 2) == iota((16, n, 32), 0) + first
            return jnp.where(hit, 1.0, 0.0).reshape(16 * n, 32)

        return jnp.concatenate([rows(32), rows(16)], axis=0).astype(BF)

    first_half, second_half, either = selector(0), selector(16), selector(0) + selector(16)
    r = iota((16, 32, 256), 1)
    want_main = (r >> 3) * 16 + (r & 7) - 16 * (iota((16, 32, 256), 2) >> 6)
    r = iota((16, 16, 256), 1)
    want_tail = (r >> 2) * 16 + 8 + (r & 3) - 16 * (iota((16, 16, 256), 2) >> 6)
    wanted = jnp.concatenate([want_main.reshape(512, 256), want_tail.reshape(256, 256)], axis=0).astype(F32)

    def spread(t, src, to):
        def one(i, carry):
            for c in range(3):
                u, v, who = plane_peer(c, nearest(i))
                remote(src[c].at[u * 4 + v], to(c), sl_s.at[t, c], sl_r.at[t, c], who, d).start()
            return carry

        lax.fori_loop(0, 15, one, 0)
        for c in range(3):
            pltpu.make_async_copy(src[c].at[plane_me[c]], to(c), sl_l.at[t, c]).start()

    above, below = [], []
    for c in range(3):
        wait_bytes(pw4.at[c, pl.ds(0, 3)], pw_r.at[c])
        heard = [pw4[c, s].astype(F32) for s in range(4)]
        above.append(jnp.concatenate([v[:, :64] for v in heard], axis=1).astype(BF))
        below.append(jnp.concatenate([v[:, 64:] for v in heard], axis=1).astype(BF))
        found = dot(first_half, above[c], 1, 0)
        p4s[c] = jnp.where(found == wanted, 1.0, 0.0).astype(BF)
    for c in range(3):
        wait_bytes(t4[c].at[pl.ds(0, 3)], ag_r.at[0, c])
        rows = dot(p4s[c, :512], t4[c][...].reshape(256, WIDTH[0][c]), 1, 0).astype(BF)
        s_main[0][c].reshape(512, WIDTH[0][c])[...] = rows
    spread(0, s_main[0], lambda c: main_rows(x5, 0, c, *plane_uv[c]))
    slot_weights = []
    for c in range(3):
        named = dot(either, below[c], 1, 0) + dot(second_half, above[c], 1, 0)
        slot_weights.append(jnp.sum(p4s[c].astype(F32) * named, axis=1, keepdims=True))
    for c in range(3):
        wait_bytes(g4[c].at[pl.ds(0, 3)], ag_r.at[1, c])
        rows = dot(p4s[c, :512], g4[c][...].reshape(256, WIDTH[1][c]), 1, 0)
        s_main[1][c].reshape(512, WIDTH[1][c])[...] = (slot_weights[c][:512] * rows).astype(BF)
    spread(1, s_main[1], lambda c: main_rows(d5, 1, c, *plane_uv[c]))
    for c in range(3):
        rows = dot(p4s[c, 512:], t4[c][...].reshape(256, WIDTH[0][c]), 1, 0).astype(BF)
        s_tail[0][c].reshape(256, WIDTH[0][c])[...] = rows
    spread(2, s_tail[0], lambda c: tail_rows(x5, xe, 0, c, *plane_uv[c]))
    for c in range(3):
        rows = dot(p4s[c, 512:], g4[c][...].reshape(256, WIDTH[1][c]), 1, 0)
        s_tail[1][c].reshape(256, WIDTH[1][c])[...] = (slot_weights[c][512:] * rows).astype(BF)
    spread(3, s_tail[1], lambda c: tail_rows(d5, de, 1, c, *plane_uv[c]))

    def moved(v, c):
        if c == 1:
            return (v & 0xC3) | ((v >> 2) & 0x0C) | ((v << 2) & 0x30)
        return ((v & 0x0C) << 4) | ((v & 0xF0) >> 2) | (v & 3)

    def arrived(t, src):
        for c in range(3):
            wait_bytes(src[c].at[pl.ds(0, 15)], sl_r.at[t, c])
            wait_bytes(src[c].at[0], sl_l.at[t, c])

    def order_tail(to, sides, t):
        for c in (1, 2):
            order = jnp.where(iota((256, 256), 0) == moved(iota((256, 256), 1), c), 1.0, 0.0).astype(BF)
            to.reshape(768, D)[512:768, FIRST[t][c] : FIRST[t][c] + WIDTH[t][c]] = dot(
                order, sides[c][...].reshape(256, WIDTH[t][c]), 1, 0
            ).astype(BF)

    def forward(i, carry):
        rows = pl.ds(pl.multiple_of(i * 256, 256), 256)
        token_rows = x5.reshape(768, D)[rows, :]
        pre = dot(token_rows, wgu[...], 1, 0)
        gate, up = pre[:, :FF], pre[:, FF:]
        sig = sigmoid(gate)
        silu = gate * sig
        hid[rows, :] = (silu * up).astype(BF)
        act[rows, :] = silu
        fac[rows, :] = up * sig * (1.0 + gate * (1.0 - sig))
        return carry

    def backward(i, carry):
        rows = pl.ds(pl.multiple_of(i * 256, 256), 256)
        grad_hidden = dot(d5.reshape(768, D)[rows, :], wd[...], 1, 1)
        ggu[rows, :FF] = (grad_hidden * fac[rows, :]).astype(BF)
        ggu[rows, FF:] = (grad_hidden * act[rows, :]).astype(BF)
        g5.reshape(768, D)[rows, :] = dot(ggu[rows, :], wgu[...], 1, 1).astype(BF)
        return carry

    def give_back(t, dst, rows_of):
        def one(i, carry):
            for c in range(3):
                u, v, who = plane_peer(c, nearest(i))
                remote(rows_of(c, u, v), dst[c].at[plane_me[c]], rt_s.at[t, c], rt_r.at[t, c], who, d).start()
            return carry

        lax.fori_loop(0, 15, one, 0)
        for c in range(3):
            pltpu.make_async_copy(rows_of(c, *plane_uv[c]), dst[c].at[plane_me[c]], rt_l.at[t, c]).start()

    wait_bytes(wgu_half, wt_r.at[0])
    wait_bytes(wd_half, wt_r.at[1])
    arrived(0, s_main[0])
    lax.fori_loop(0, 2, forward, 0)
    arrived(1, s_main[1])
    lax.fori_loop(0, 2, backward, 0)
    give_back(0, r_main, lambda c, u, v: main_rows(g5, 2, c, u, v))

    arrived(2, s_tail[0])
    order_tail(x5, xe, 0)
    lax.fori_loop(2, 3, forward, 0)
    arrived(3, s_tail[1])
    order_tail(d5, de, 1)
    lax.fori_loop(2, 3, backward, 0)
    for c in (1, 2):
        order = jnp.where(moved(iota((256, 256), 0), c) == iota((256, 256), 1), 1.0, 0.0).astype(BF)
        ge[c].reshape(256, WIDTH[2][c])[...] = dot(
            order, g5.reshape(768, D)[512:768, FIRST[2][c] : FIRST[2][c] + WIDTH[2][c]], 1, 0
        ).astype(BF)
    give_back(1, r_tail, lambda c, u, v: tail_rows(g5, ge, 2, c, u, v))

    def sums_in(j, carry):
        wide = pl.ds(pl.multiple_of(j * 512, 512), 512)
        grads = dot(x5.reshape(768, D)[:, wide], ggu[...], 0, 0)
        for g in range(4):
            low = logu[pl.ds(j * 4 + g, 1), :]
            grad = grads[g * 128 : (g + 1) * 128]
            value = wgu[pl.ds(j * 512 + g * 128, 128), :].astype(F32)
            at = pl.ds((j % 2) * 4 + g, 1)
            sbi[j // 2, 0, at, :] = jnp.sum(grad * (value + low), axis=0, keepdims=True)
            sbi[j // 2, 1, at, :] = jnp.sum(grad, axis=0, keepdims=True)
        return carry

    lax.fori_loop(0, 4, sums_in, 0)
    sbi_out = sbi.at[other]
    remote(sbi_out, rbi, sm_s.at[0], sm_r.at[0], e, other).start()

    def sums_out(j, carry):
        wide = pl.ds(pl.multiple_of(j * 512, 512), 512)
        grads = dot(hid[...], d5.reshape(768, D)[:, wide], 0, 0)
        low = loo[:, wide]
        total = [[jnp.zeros((1, 512), F32)] * 6, [jnp.zeros((1, 512), F32)] * 6]
        for k, r0, groups in down_blocks():
            grad = grads[k * 256 + r0 : k * 256 + r0 + 32]
            value = wd[k * 256 + r0 : k * 256 + r0 + 32, wide].astype(F32)
            unit = iota((32, 512), 0)
            for g, first, last in groups:
                mine = grad
                if len(groups) > 1:
                    mine = jnp.where((unit >= first) & (unit < last), grad, 0.0)
                total[0][g] = total[0][g] + jnp.sum(mine * (value + low[g][None]), axis=0, keepdims=True)
                total[1][g] = total[1][g] + jnp.sum(mine, axis=0, keepdims=True)
        at = pl.ds(pl.multiple_of((j % 2) * 512, 512), 512)
        for t in range(2):
            for g in range(6):
                sbo[j // 2, t, g : g + 1, at] = total[t][g]
        return carry

    lax.fori_loop(0, 4, sums_out, 0)
    sbo_out = sbo.at[other]
    remote(sbo_out, rbo, sm_s.at[1], sm_r.at[1], e, other).start()

    wait_bytes(rbi, sm_r.at[0])
    share = pl.ds(pl.multiple_of(d * 8, 8), 8)
    upper_sum = (sbi[d, 0] + rbi[0]) / (upgu[share, :] + logu[share, :])
    lower_sum = upper_sum - (sbi[d, 1] + rbi[1])
    totals = [total[:, p * FF : (p + 1) * FF] for p in range(2) for total in (upper_sum, lower_sum)]
    plain = join3(dot(split3(jnp.concatenate(totals, axis=0)), nibble_order(), 1, 1))
    for p in range(2):
        for t in range(2):
            sig = sigmoid(clinv[p, t, share, :])
            total = plain[(p * 2 + t) * 8 : (p * 2 + t) * 8 + 8]
            o_in[0, p, t] = total * rginv[p, t, share, :] * sig * (1.0 - sig)
    wait_bytes(rbo, sm_r.at[1])
    span = upo[:, half] + loo[:, half]
    upper_out = (sbo[d, 0] + rbo[0])[:6] / span
    lower_out = upper_out - (sbo[d, 1] + rbo[1])[:6]
    for g in range(6):
        sig = sigmoid(cloutv[g, :, half])
        total = jnp.concatenate([upper_out[g : g + 1], lower_out[g : g + 1]], axis=0)
        o_out[g] = total * rgoutv[g, :, half] * sig * (1.0 - sig)

    sums = []
    for c in range(3):
        wait_bytes(r_main[c].at[pl.ds(0, 15)], rt_r.at[0, c])
        wait_bytes(r_main[c].at[0], rt_l.at[0, c])
        sums.append(dot(p4s[c, :512], r_main[c].reshape(512, WIDTH[2][c])[...], 0, 0))
    for c in range(3):
        wait_bytes(r_tail[c].at[pl.ds(0, 15)], rt_r.at[1, c])
        wait_bytes(r_tail[c].at[0], rt_l.at[1, c])
        total = sums[c] + dot(p4s[c, 512:], r_tail[c].reshape(256, WIDTH[2][c])[...], 0, 0)
        part[c][...] = total.astype(BF).reshape(4, TOK, WIDTH[2][c])
        for k in (2, 1, 3):
            s, who = line_peer(c, k)
            remote(part[c].at[s], got[c].at[here[c]], pt_s.at[c], pt_r.at[c], who, d).start()
    for c in range(3):
        wait_bytes(got[c].at[pl.ds(0, 3)], pt_r.at[c])
        total = part[c][here[c]].astype(F32)
        for k in (1, 2, 3):
            s, _ = line_peer(c, k)
            total = total + got[c][s].astype(F32)
        o_tok[:, cols[2][c]] = total.astype(BF)

    for c in range(3):
        wait_bytes(pw4.at[c, pl.ds(0, 3)], pw_s.at[c])
        wait_bytes(t4[c].at[pl.ds(0, 3)], ag_s.at[0, c])
        wait_bytes(g4[c].at[pl.ds(0, 3)], ag_s.at[1, c])
        for t in range(2):
            wait_bytes(s_main[t][c].at[pl.ds(0, 15)], sl_s.at[t, c])
            wait_bytes(s_tail[t][c].at[pl.ds(0, 15)], sl_s.at[2 + t, c])
        wait_bytes(r_main[c].at[pl.ds(0, 15)], rt_s.at[0, c])
        wait_bytes(r_tail[c].at[pl.ds(0, 15)], rt_s.at[1, c])
        wait_bytes(got[c].at[pl.ds(0, 3)], pt_s.at[c])
    wait_bytes(wgu_half, wt_s.at[0])
    wait_bytes(wd_half, wt_s.at[1])
    wait_bytes(sbi_out, sm_s.at[0])
    wait_bytes(sbo_out, sm_s.at[1])


def hand_out(a, b, c, to_a, to_b, to_c):
    to_a[...] = a[...]
    to_b[...] = b[...]
    to_c[...] = c[...]


def body(tokens, grad_out, expert_ids, router_weights, codes_in, codes_out, clip_in, range_in, clip_out, range_out):
    def vm(*shape, t=BF):
        return pltpu.VMEM(shape, t)

    dma = pltpu.SemaphoreType.DMA
    tok_w, slope_w, back_w = WIDTH
    scratch = [vm(12, 32, 128)]
    scratch += [vm(4, TOK, w) for w in tok_w + slope_w] + [vm(3, 4, 32, 128)]
    scratch += [vm(16, 4, 8, w) for w in tok_w + slope_w] + [vm(16, 2, 8, w) for w in tok_w + slope_w]
    scratch += [vm(6, 4, 4, 8, D)] * 3
    scratch += [vm(16, 2, 8, w) for w in tok_w[1:] + slope_w[1:] + back_w[1:]]
    scratch += [vm(16, 4, 8, w) for w in back_w] + [vm(16, 2, 8, w) for w in back_w] + [vm(3, 768, 256)]
    scratch += [vm(D, 2 * FF), vm(FF, D), vm(16, 2 * FF, t=F32), vm(16, 2 * FF, t=F32), vm(6, D, t=F32), vm(6, D, t=F32)]
    scratch += [vm(2, 1024, 256, t=I32), vm(256, 1024, t=I32), vm(8, TOK, t=I32), vm(8, TOK, t=F32)]
    scratch += [vm(2, 2, 16, FF, t=F32)] * 2 + [vm(6, 2, D, t=F32)] * 2
    scratch += [vm(768, FF), vm(768, 2 * FF), vm(768, FF, t=F32), vm(768, FF, t=F32)]
    scratch += [vm(4, TOK, w) for w in back_w] * 2
    scratch += [vm(2, 2, 8, 2 * FF, t=F32), vm(2, 2, 8, 1024, t=F32), vm(2, 8, 2 * FF, t=F32), vm(2, 8, 1024, t=F32)]
    scratch += [dma((14,)), dma((2, 3)), dma((2, 3)), dma((3,)), dma((3,)), dma((4, 3)), dma((4, 3)), dma((4, 3))]
    scratch += [dma((2, 3)), dma((2, 3)), dma((2, 3)), dma((3,)), dma((3,)), dma((2,)), dma((2,)), dma((2,)), dma((2,))]
    args = (
        tokens, grad_out, expert_ids.T, router_weights.T, codes_in[0], codes_out[0],
        clip_in[0], range_in[0], clip_out[0].transpose(1, 0, 2), range_out[0].transpose(1, 0, 2),
    )
    vmem, anywhere = pl.BlockSpec(memory_space=pltpu.VMEM), pl.BlockSpec(memory_space=pl.ANY)
    results = (
        jax.ShapeDtypeStruct((TOK, D), BF),
        jax.ShapeDtypeStruct((1, 2, 2, 8, FF), F32),
        jax.ShapeDtypeStruct((6, 2, 1024), F32),
    )
    found = pl.pallas_call(
        kernel,
        out_shape=tuple(pltpu.VMEM(v.shape, v.dtype) for v in results),
        in_specs=[anywhere] * len(args),
        out_specs=(vmem,) * 3,
        scratch_shapes=scratch,
        compiler_params=pltpu.CompilerParams(collective_id=0, has_side_effects=True, vmem_limit_bytes=62 << 20),
    )(*args)
    grad_tokens, grad_in, grad_out_clip = pl.pallas_call(
        hand_out, out_shape=results, in_specs=[vmem] * 3, out_specs=(vmem,) * 3
    )(*(pltpu.with_memory_space_constraint(v, pltpu.VMEM) for v in found))
    return grad_tokens, grad_in, grad_out_clip.transpose(1, 0, 2)[None]


def solution(mesh):
    return jax.shard_map(
        body,
        mesh=mesh,
        in_specs=(
            P(("expert", "dp"), None),
            P(("expert", "dp"), None),
            P(("expert", "dp"), None),
            P(("expert", "dp"), None),
            P("expert", None, "dp", None),
            P("expert", None, "dp"),
            P("expert", None, None, None, None),
            P("expert", None, None, None, None),
            P("expert", None, None, None),
            P("expert", None, None, None),
        ),
        out_specs=(
            P(("expert", "dp"), None),
            P("expert", None, None, "dp", None),
            P("expert", None, None, "dp"),
        ),
        check_vma=False,
    )
```

```python
import functools

import jax
import jax.numpy as jnp
from jax import lax
from jax.experimental import pallas as pl
from jax.experimental.pallas import tpu as pltpu
from jax.sharding import PartitionSpec as P

MESH = pl.DeviceIdType.MESH
D, FF, TOK = 2048, 768, 64
WIDTH = ((640, 640, 768), (640, 768, 640), (768, 640, 640))
FIRST = ((0, 640, 1280), (0, 640, 1408), (0, 768, 1408))
BF, F32, I32 = jnp.bfloat16, jnp.float32, jnp.int32
HI = lax.Precision.HIGHEST


def dot(a, b, da, db, **kw):
    return lax.dot_general(a, b, (((da,), (db,)), ((), ())), preferred_element_type=F32, **kw)


def iota(shape, dim):
    return lax.broadcasted_iota(I32, shape, dim)


def sigmoid(v):
    return 1.0 / (1.0 + jnp.exp(-v))


def down_blocks():
    out = []
    for k in range(3):
        for block in range(8):
            rows = range(block * 32, block * 32 + 32)
            groups = {}
            for r in rows:
                groups.setdefault((3 * r + k) // 128, []).append(r - block * 32)
            out.append((k, block * 32, [(g, min(v), max(v) + 1) for g, v in sorted(groups.items())]))
    return out


def split3(v):
    high = v.astype(BF)
    rest = v - high.astype(F32)
    mid = rest.astype(BF)
    low = (rest - mid.astype(F32)).astype(BF)
    return jnp.concatenate([high, mid, low], axis=0)


def join3(v):
    n = v.shape[0] // 3
    return (v[2 * n :] + v[n : 2 * n]) + v[:n]


def nibble_order():
    return jnp.where(
        iota((FF, FF), 0) == 3 * (iota((FF, FF), 1) & 255) + (iota((FF, FF), 1) >> 8), 1.0, 0.0
    ).astype(BF)


def kernel(
    tok, go, ids, rw, cin, cout, clin, rgin, clout, rgout,
    o_tok, o_in, o_out,
    tab, t4a, t4b, t4c, g4a, g4b, g4c, pw4,
    sma, smb, smc, dma_, dmb, dmc, sxa, sxb, sxc, dxa, dxb, dxc,
    x5, d5, g5, xeb, xec, deb, dec, geb, gec,
    rma, rmb, rmc, rxa, rxb, rxc, p4s, p4t, ta, tb, tc,
    wgu, wd, upgu, logu, upo, loo, cinv, coutv, idv, rwv, clinv, rginv, cloutv, rgoutv,
    hid, ggu, fac, act, qa, qb, qc, ha, hb, hc,
    sbi, sbo, rbi, rbo,
    in_l, ag_s, ag_r, pw_s, pw_r, sl_s, sl_r, sl_l, rt_s, rt_r, rt_l, pt_s, pt_r, wt_s, wt_r, sm_s, sm_r,
):
    e, d = lax.axis_index("expert"), lax.axis_index("dp")
    z, y, x = e // 16, (e // 4) % 4, e % 4
    here = (x, y, z)
    t4, g4 = (t4a, t4b, t4c), (g4a, g4b, g4c)
    s_main, s_tail = ((sma, smb, smc), (dma_, dmb, dmc)), ((sxa, sxb, sxc), (dxa, dxb, dxc))
    xe, de, ge = (None, xeb, xec), (None, deb, dec), (None, geb, gec)
    r_main, r_tail = (rma, rmb, rmc), (rxa, rxb, rxc)
    part, got = (qa, qb, qc), (ha, hb, hc)
    cols = [[pl.ds(FIRST[t][c], WIDTH[t][c]) for c in range(3)] for t in range(3)]

    def expert_at(zz, yy, xx):
        return zz * 16 + yy * 4 + xx

    def line_peer(c, k):
        s = (here[c] + k) % 4
        return s, (expert_at(z, y, s), expert_at(z, s, x), expert_at(s, y, x))[c]

    def plane_peer(c, o):
        a, b = o // 4, o % 4
        u, v = ((z, y), (z, x), (y, x))[c]
        u, v = (u + a) % 4, (v + b) % 4
        return u, v, (expert_at(u, v, x), expert_at(u, y, v), expert_at(z, u, v))[c]

    def nearest(i):
        return jnp.where(i < 7, 0x8DF134C >> (4 * jnp.minimum(i, 6)), 0x6A9BE257 >> (4 * jnp.maximum(i - 7, 0))) & 15

    def main_rows(ref, t, c, u, v):
        if c == 0:
            return ref.at[u, v, :, :, cols[t][c]]
        if c == 1:
            return ref.at[u, :, v, :, cols[t][c]]
        return ref.at[pl.ds(0, 4), u, v, :, cols[t][c]]

    def tail_rows(ref, sides, t, c, u, v):
        if c == 0:
            return ref.at[4 + u // 2, (u % 2) * 2 + v // 2, pl.ds((v % 2) * 2, 2), :, cols[t][c]]
        return sides[c].at[u * 4 + v]

    def remote(src, dst, s, r, who, core):
        return pltpu.make_async_remote_copy(
            src_ref=src, dst_ref=dst, send_sem=s, recv_sem=r, device_id=(who, core), device_id_type=MESH
        )

    def wait_bytes(ref, sem):
        pltpu.make_async_copy(ref, ref, sem).wait()

    plane_me = (z * 4 + y, z * 4 + x, y * 4 + x)
    plane_uv = ((z, y), (z, x), (y, x))

    barrier = pltpu.get_barrier_semaphore()
    for c in range(3):
        for k in (2, 1, 3):
            pl.semaphore_signal(barrier, inc=1, device_id=(line_peer(c, k)[1], d), device_id_type=MESH)
    pl.semaphore_signal(barrier, inc=1, device_id=(e, 1 - d), device_id_type=MESH)

    small = [(ids, idv), (rw, rwv), (clin, clinv), (rgin, rginv), (clout, cloutv), (rgout, rgoutv), (cin, cinv), (cout, coutv)]
    loads = [pltpu.make_async_copy(src, dst, in_l.at[6 + i]) for i, (src, dst) in enumerate(small)]
    loads[0].start()
    loads[1].start()
    for c in range(3):
        pltpu.make_async_copy(tok.at[:, cols[0][c]], t4[c].at[here[c]], in_l.at[c]).start()
    for c in range(3):
        pltpu.make_async_copy(go.at[:, cols[1][c]], g4[c].at[here[c]], in_l.at[3 + c]).start()
    for load in loads[2:]:
        load.start()
    loads[0].wait()
    loads[1].wait()

    row = iota((128, TOK), 0)
    chosen = jnp.zeros((128, TOK), F32)
    weight = jnp.zeros((128, TOK), F32)
    for k in range(8):
        ident = idv[k : k + 1, :]
        chosen = chosen + jnp.where(row == ident, 1.0, 0.0)
        weight = weight + jnp.where(row == ident + 64, rwv[k : k + 1, :], 0.0)
    earlier = jnp.where(iota((TOK, TOK), 0) < iota((TOK, TOK), 1), 1.0, 0.0).astype(BF)
    before = dot(chosen.astype(BF), earlier, 1, 0)
    rank = jnp.where(chosen > 0.5, before, jnp.where(row < 64, -64.0, 0.0))
    table = rank + weight
    high = table.astype(BF).astype(F32)
    left = table - high
    mid = left.astype(BF).astype(F32)
    low = left - mid
    table = jnp.concatenate([high, jnp.concatenate([low[64:], mid[64:]], axis=0)], axis=1).astype(BF)
    plans = []
    for c in range(3):
        s, i = iota((4, 32, 128), 0), iota((4, 32, 128), 1)
        u, v = (i >> 2) & 3, i & 3
        named = (expert_at(u, v, s), expert_at(u, s, v), expert_at(s, u, v))[c] + (i >> 4) * 64
        plans.append(jnp.where(iota((4, 32, 128), 2) == named, 1.0, 0.0).reshape(128, 128))
    plans = jnp.concatenate(plans, axis=0).astype(BF)
    tab.reshape(384, 128)[...] = dot(plans, table, 1, 0).astype(BF)
    for c in range(3):
        pw4[c, here[c]] = tab[c * 4 + here[c]]

    for c in range(3):
        wait_bytes(t4[c].at[here[c]], in_l.at[c])
        wait_bytes(g4[c].at[here[c]], in_l.at[3 + c])
    pl.semaphore_wait(barrier, 10)

    for k in (2, 1, 3):
        for c in range(3):
            at, who = line_peer(c, k)
            remote(tab.at[c * 4 + at], pw4.at[c, here[c]], pw_s.at[c], pw_r.at[c], who, d).start()
    for t, q4 in enumerate((t4, g4)):
        for k in (2, 1, 3):
            for c in range(3):
                _, who = line_peer(c, k)
                mine = q4[c].at[here[c]]
                remote(mine, mine, ag_s.at[t, c], ag_r.at[t, c], who, d).start()

    for load in loads[2:]:
        load.wait()
    ends = [sigmoid(clinv[p, t]) * rginv[p, t] for p in range(2) for t in range(2)]
    ends = join3(dot(split3(jnp.concatenate(ends, axis=0)), nibble_order(), 1, 0))
    for p in range(2):
        upgu[:, p * FF : (p + 1) * FF] = ends[p * 32 : p * 32 + 16]
        logu[:, p * FF : (p + 1) * FF] = ends[p * 32 + 16 : p * 32 + 32]
    for g in range(6):
        end = sigmoid(cloutv[g]) * rgoutv[g]
        upo[g : g + 1, :] = end[0:1]
        loo[g : g + 1, :] = end[1:2]

    def dequant_in(g, carry):
        up = upgu[pl.ds(d * 8 + g, 1), :]
        lo = logu[pl.ds(d * 8 + g, 1), :]
        step = (up + lo) / 15.0
        for p in range(2):
            words = cinv[p, pl.ds(g * 128, 128), :]
            for k in range(3):
                c0 = p * FF + k * 256
                code = ((words >> (4 * k)) & 15).astype(F32)
                wgu[pl.ds(d * 1024 + g * 128, 128), c0 : c0 + 256] = (
                    code * step[:, c0 : c0 + 256] - lo[:, c0 : c0 + 256]
                ).astype(BF)
        return carry

    lax.fori_loop(0, 8, dequant_in, 0)
    half = pl.ds(pl.multiple_of(d * 1024, 1024), 1024)
    up_half, lo_half = upo[:, half], loo[:, half]
    step_half = (up_half + lo_half) / 15.0
    for k, r0, groups in down_blocks():
        code = ((coutv[r0 : r0 + 32, :] >> (4 * k)) & 15).astype(F32)
        unit = iota((32, 1024), 0)
        scale, shift = step_half[groups[0][0]][None], lo_half[groups[0][0]][None]
        for g, first, _ in groups[1:]:
            scale = jnp.where(unit >= first, step_half[g][None], scale)
            shift = jnp.where(unit >= first, lo_half[g][None], shift)
        wd[k * 256 + r0 : k * 256 + r0 + 32, half] = (code * scale - shift).astype(BF)

    other = 1 - d
    wgu_half = wgu.at[pl.ds(pl.multiple_of(d * 1024, 1024), 1024), :]
    wd_half = wd.at[:, half]
    remote(wgu_half, wgu_half, wt_s.at[0], wt_r.at[0], e, other).start()
    remote(wd_half, wd_half, wt_s.at[1], wt_r.at[1], e, other).start()

    def selector(first):
        def rows(n):
            hit = iota((16, n, 32), 2) == iota((16, n, 32), 0) + first
            return jnp.where(hit, 1.0, 0.0).reshape(16 * n, 32)

        return jnp.concatenate([rows(32), rows(16)], axis=0).astype(BF)

    first_half, second_half, either = selector(0), selector(16), selector(0) + selector(16)
    r = iota((16, 32, 256), 1)
    want_main = (r >> 3) * 16 + (r & 7) - 16 * (iota((16, 32, 256), 2) >> 6)
    r = iota((16, 16, 256), 1)
    want_tail = (r >> 2) * 16 + 8 + (r & 3) - 16 * (iota((16, 16, 256), 2) >> 6)
    wanted = jnp.concatenate([want_main.reshape(512, 256), want_tail.reshape(256, 256)], axis=0).astype(F32)

    def spread(t, src, to, first=0, last=15, ranges=(0, 1, 2)):
        def one(i, carry):
            for c in ranges:
                u, v, who = plane_peer(c, nearest(i))
                remote(src[c].at[u * 4 + v], to(c), sl_s.at[t, c], sl_r.at[t, c], who, d).start()
            return carry

        lax.fori_loop(first, last, one, 0)
        if last == 15:
            for c in ranges:
                pltpu.make_async_copy(src[c].at[plane_me[c]], to(c), sl_l.at[t, c]).start()

    above, below = [], []
    for c in range(3):
        wait_bytes(pw4.at[c, pl.ds(0, 3)], pw_r.at[c])
        heard = [pw4[c, s].astype(F32) for s in range(4)]
        above.append(jnp.concatenate([v[:, :64] for v in heard], axis=1).astype(BF))
        below.append(jnp.concatenate([v[:, 64:] for v in heard], axis=1).astype(BF))
        found = dot(first_half, above[c], 1, 0)
        p4s[c] = jnp.where(found == wanted, 1.0, 0.0).astype(BF)
    for c in range(3):
        wait_bytes(t4[c].at[pl.ds(0, 3)], ag_r.at[0, c])
        rows = dot(p4s[c, :512], t4[c][...].reshape(256, WIDTH[0][c]), 1, 0).astype(BF)
        s_main[0][c].reshape(512, WIDTH[0][c])[...] = rows
        spread(0, s_main[0], lambda c: main_rows(x5, 0, c, *plane_uv[c]), 0, 4, (c,))
    spread(0, s_main[0], lambda c: main_rows(x5, 0, c, *plane_uv[c]), 4)
    slot_weights = []
    for c in range(3):
        named = dot(either, below[c], 1, 0) + dot(second_half, above[c], 1, 0)
        slot_weights.append(jnp.sum(p4s[c].astype(F32) * named, axis=1, keepdims=True))
    for c in range(3):
        wait_bytes(g4[c].at[pl.ds(0, 3)], ag_r.at[1, c])
        rows = dot(p4s[c, :512], g4[c][...].reshape(256, WIDTH[1][c]), 1, 0)
        s_main[1][c].reshape(512, WIDTH[1][c])[...] = (slot_weights[c][:512] * rows).astype(BF)
    spread(1, s_main[1], lambda c: main_rows(d5, 1, c, *plane_uv[c]))
    for c in range(3):
        rows = dot(p4s[c, 512:], t4[c][...].reshape(256, WIDTH[0][c]), 1, 0).astype(BF)
        s_tail[0][c].reshape(256, WIDTH[0][c])[...] = rows
    spread(2, s_tail[0], lambda c: tail_rows(x5, xe, 0, c, *plane_uv[c]))
    for c in range(3):
        rows = dot(p4s[c, 512:], g4[c][...].reshape(256, WIDTH[1][c]), 1, 0)
        s_tail[1][c].reshape(256, WIDTH[1][c])[...] = (slot_weights[c][512:] * rows).astype(BF)
    spread(3, s_tail[1], lambda c: tail_rows(d5, de, 1, c, *plane_uv[c]))

    def moved(v, c):
        if c == 1:
            return (v & 0xC3) | ((v >> 2) & 0x0C) | ((v << 2) & 0x30)
        return ((v & 0x0C) << 4) | ((v & 0xF0) >> 2) | (v & 3)

    def arrived(t, src):
        for c in range(3):
            wait_bytes(src[c].at[pl.ds(0, 15)], sl_r.at[t, c])
            wait_bytes(src[c].at[0], sl_l.at[t, c])

    def order_tail(to, sides, t):
        for c in (1, 2):
            order = jnp.where(iota((256, 256), 0) == moved(iota((256, 256), 1), c), 1.0, 0.0).astype(BF)
            to.reshape(768, D)[512:768, FIRST[t][c] : FIRST[t][c] + WIDTH[t][c]] = dot(
                order, sides[c][...].reshape(256, WIDTH[t][c]), 1, 0
            ).astype(BF)

    def forward(i, carry):
        rows = pl.ds(pl.multiple_of(i * 256, 256), 256)
        token_rows = x5.reshape(768, D)[rows, :]
        pre = dot(token_rows, wgu[...], 1, 0)
        gate, up = pre[:, :FF], pre[:, FF:]
        sig = sigmoid(gate)
        silu = gate * sig
        hid[rows, :] = (silu * up).astype(BF)
        act[rows, :] = silu
        fac[rows, :] = up * sig * (1.0 + gate * (1.0 - sig))
        return carry

    def backward(i, carry):
        rows = pl.ds(pl.multiple_of(i * 256, 256), 256)
        grad_hidden = dot(d5.reshape(768, D)[rows, :], wd[...], 1, 1)
        ggu[rows, :FF] = (grad_hidden * fac[rows, :]).astype(BF)
        ggu[rows, FF:] = (grad_hidden * act[rows, :]).astype(BF)
        g5.reshape(768, D)[rows, :] = dot(ggu[rows, :], wgu[...], 1, 1).astype(BF)
        return carry

    def give_back(t, dst, rows_of):
        def one(i, carry):
            for c in range(3):
                u, v, who = plane_peer(c, nearest(i))
                remote(rows_of(c, u, v), dst[c].at[plane_me[c]], rt_s.at[t, c], rt_r.at[t, c], who, d).start()
            return carry

        lax.fori_loop(0, 15, one, 0)
        for c in range(3):
            pltpu.make_async_copy(rows_of(c, *plane_uv[c]), dst[c].at[plane_me[c]], rt_l.at[t, c]).start()

    for c in range(3):
        p4t[c] = p4s[c].T
    wait_bytes(wgu_half, wt_r.at[0])
    wait_bytes(wd_half, wt_r.at[1])
    arrived(0, s_main[0])
    lax.fori_loop(0, 2, forward, 0)
    arrived(1, s_main[1])
    lax.fori_loop(0, 2, backward, 0)
    give_back(0, r_main, lambda c, u, v: main_rows(g5, 2, c, u, v))

    arrived(2, s_tail[0])
    order_tail(x5, xe, 0)
    lax.fori_loop(2, 3, forward, 0)
    arrived(3, s_tail[1])
    order_tail(d5, de, 1)
    lax.fori_loop(2, 3, backward, 0)
    for c in (1, 2):
        order = jnp.where(moved(iota((256, 256), 0), c) == iota((256, 256), 1), 1.0, 0.0).astype(BF)
        ge[c].reshape(256, WIDTH[2][c])[...] = dot(
            order, g5.reshape(768, D)[512:768, FIRST[2][c] : FIRST[2][c] + WIDTH[2][c]], 1, 0
        ).astype(BF)
    give_back(1, r_tail, lambda c, u, v: tail_rows(g5, ge, 2, c, u, v))

    def sums_in(j, carry):
        wide = pl.ds(pl.multiple_of(j * 512, 512), 512)
        grads = dot(x5.reshape(768, D)[:, wide], ggu[...], 0, 0)
        for g in range(4):
            low = logu[pl.ds(j * 4 + g, 1), :]
            grad = grads[g * 128 : (g + 1) * 128]
            value = wgu[pl.ds(j * 512 + g * 128, 128), :].astype(F32)
            at = pl.ds((j % 2) * 4 + g, 1)
            sbi[j // 2, 0, at, :] = jnp.sum(grad * (value + low), axis=0, keepdims=True)
            sbi[j // 2, 1, at, :] = jnp.sum(grad, axis=0, keepdims=True)
        return carry

    lax.fori_loop(0, 4, sums_in, 0)
    sbi_out = sbi.at[other]
    remote(sbi_out, rbi, sm_s.at[0], sm_r.at[0], e, other).start()

    def sums_out(j, carry):
        wide = pl.ds(pl.multiple_of(j * 512, 512), 512)
        grads = dot(hid[...], d5.reshape(768, D)[:, wide], 0, 0)
        low = loo[:, wide]
        total = [[jnp.zeros((1, 512), F32)] * 6, [jnp.zeros((1, 512), F32)] * 6]
        for k, r0, groups in down_blocks():
            grad = grads[k * 256 + r0 : k * 256 + r0 + 32]
            value = wd[k * 256 + r0 : k * 256 + r0 + 32, wide].astype(F32)
            unit = iota((32, 512), 0)
            for g, first, last in groups:
                mine = grad
                if len(groups) > 1:
                    mine = jnp.where((unit >= first) & (unit < last), grad, 0.0)
                total[0][g] = total[0][g] + jnp.sum(mine * (value + low[g][None]), axis=0, keepdims=True)
                total[1][g] = total[1][g] + jnp.sum(mine, axis=0, keepdims=True)
        at = pl.ds(pl.multiple_of((j % 2) * 512, 512), 512)
        for t in range(2):
            for g in range(6):
                sbo[j // 2, t, g : g + 1, at] = total[t][g]
        return carry

    lax.fori_loop(0, 4, sums_out, 0)
    sbo_out = sbo.at[other]
    remote(sbo_out, rbo, sm_s.at[1], sm_r.at[1], e, other).start()

    wait_bytes(rbi, sm_r.at[0])
    share = pl.ds(pl.multiple_of(d * 8, 8), 8)
    upper_sum = (sbi[d, 0] + rbi[0]) / (upgu[share, :] + logu[share, :])
    lower_sum = upper_sum - (sbi[d, 1] + rbi[1])
    totals = [total[:, p * FF : (p + 1) * FF] for p in range(2) for total in (upper_sum, lower_sum)]
    plain = join3(dot(split3(jnp.concatenate(totals, axis=0)), nibble_order(), 1, 1))
    for p in range(2):
        for t in range(2):
            sig = sigmoid(clinv[p, t, share, :])
            total = plain[(p * 2 + t) * 8 : (p * 2 + t) * 8 + 8]
            o_in[0, p, t] = total * rginv[p, t, share, :] * sig * (1.0 - sig)
    wait_bytes(rbo, sm_r.at[1])
    span = upo[:, half] + loo[:, half]
    upper_out = (sbo[d, 0] + rbo[0])[:6] / span
    lower_out = upper_out - (sbo[d, 1] + rbo[1])[:6]
    for g in range(6):
        sig = sigmoid(cloutv[g, :, half])
        total = jnp.concatenate([upper_out[g : g + 1], lower_out[g : g + 1]], axis=0)
        o_out[g] = total * rgoutv[g, :, half] * sig * (1.0 - sig)

    sums = (ta, tb, tc)
    for c in range(3):
        wait_bytes(r_main[c].at[pl.ds(0, 15)], rt_r.at[0, c])
        wait_bytes(r_main[c].at[0], rt_l.at[0, c])
        sums[c][...] = dot(p4t[c, :, :512], r_main[c].reshape(512, WIDTH[2][c])[...], 1, 0)
    for c in range(3):
        wait_bytes(r_tail[c].at[pl.ds(0, 15)], rt_r.at[1, c])
        wait_bytes(r_tail[c].at[0], rt_l.at[1, c])
        total = sums[c][...] + dot(p4t[c, :, 512:], r_tail[c].reshape(256, WIDTH[2][c])[...], 1, 0)
        part[c][...] = total.astype(BF).reshape(4, TOK, WIDTH[2][c])
        for k in (2, 1, 3):
            s, who = line_peer(c, k)
            remote(part[c].at[s], got[c].at[here[c]], pt_s.at[c], pt_r.at[c], who, d).start()
    for c in range(3):
        wait_bytes(got[c].at[pl.ds(0, 3)], pt_r.at[c])
        total = part[c][here[c]].astype(F32)
        for k in (1, 2, 3):
            s, _ = line_peer(c, k)
            total = total + got[c][s].astype(F32)
        o_tok[:, cols[2][c]] = total.astype(BF)

    for c in range(3):
        wait_bytes(pw4.at[c, pl.ds(0, 3)], pw_s.at[c])
        wait_bytes(t4[c].at[pl.ds(0, 3)], ag_s.at[0, c])
        wait_bytes(g4[c].at[pl.ds(0, 3)], ag_s.at[1, c])
        for t in range(2):
            wait_bytes(s_main[t][c].at[pl.ds(0, 15)], sl_s.at[t, c])
            wait_bytes(s_tail[t][c].at[pl.ds(0, 15)], sl_s.at[2 + t, c])
        wait_bytes(r_main[c].at[pl.ds(0, 15)], rt_s.at[0, c])
        wait_bytes(r_tail[c].at[pl.ds(0, 15)], rt_s.at[1, c])
        wait_bytes(got[c].at[pl.ds(0, 3)], pt_s.at[c])
    wait_bytes(wgu_half, wt_s.at[0])
    wait_bytes(wd_half, wt_s.at[1])
    wait_bytes(sbi_out, sm_s.at[0])
    wait_bytes(sbo_out, sm_s.at[1])


def hand_out(a, b, c, to_a, to_b, to_c):
    to_a[...] = a[...]
    to_b[...] = b[...]
    to_c[...] = c[...]


def body(tokens, grad_out, expert_ids, router_weights, codes_in, codes_out, clip_in, range_in, clip_out, range_out):
    def vm(*shape, t=BF):
        return pltpu.VMEM(shape, t)

    dma = pltpu.SemaphoreType.DMA
    tok_w, slope_w, back_w = WIDTH
    scratch = [vm(12, 32, 128)]
    scratch += [vm(4, TOK, w) for w in tok_w + slope_w] + [vm(3, 4, 32, 128)]
    scratch += [vm(16, 4, 8, w) for w in tok_w + slope_w] + [vm(16, 2, 8, w) for w in tok_w + slope_w]
    scratch += [vm(6, 4, 4, 8, D)] * 3
    scratch += [vm(16, 2, 8, w) for w in tok_w[1:] + slope_w[1:] + back_w[1:]]
    scratch += [vm(16, 4, 8, w) for w in back_w] + [vm(16, 2, 8, w) for w in back_w] + [vm(3, 768, 256), vm(3, 256, 768)]
    scratch += [vm(256, w, t=F32) for w in back_w]
    scratch += [vm(D, 2 * FF), vm(FF, D), vm(16, 2 * FF, t=F32), vm(16, 2 * FF, t=F32), vm(6, D, t=F32), vm(6, D, t=F32)]
    scratch += [vm(2, 1024, 256, t=I32), vm(256, 1024, t=I32), vm(8, TOK, t=I32), vm(8, TOK, t=F32)]
    scratch += [vm(2, 2, 16, FF, t=F32)] * 2 + [vm(6, 2, D, t=F32)] * 2
    scratch += [vm(768, FF), vm(768, 2 * FF), vm(768, FF, t=F32), vm(768, FF, t=F32)]
    scratch += [vm(4, TOK, w) for w in back_w] * 2
    scratch += [vm(2, 2, 8, 2 * FF, t=F32), vm(2, 2, 8, 1024, t=F32), vm(2, 8, 2 * FF, t=F32), vm(2, 8, 1024, t=F32)]
    scratch += [dma((14,)), dma((2, 3)), dma((2, 3)), dma((3,)), dma((3,)), dma((4, 3)), dma((4, 3)), dma((4, 3))]
    scratch += [dma((2, 3)), dma((2, 3)), dma((2, 3)), dma((3,)), dma((3,)), dma((2,)), dma((2,)), dma((2,)), dma((2,))]
    args = (
        tokens, grad_out, expert_ids.T, router_weights.T, codes_in[0], codes_out[0],
        clip_in[0], range_in[0], clip_out[0].transpose(1, 0, 2), range_out[0].transpose(1, 0, 2),
    )
    vmem, anywhere = pl.BlockSpec(memory_space=pltpu.VMEM), pl.BlockSpec(memory_space=pl.ANY)
    results = (
        jax.ShapeDtypeStruct((TOK, D), BF),
        jax.ShapeDtypeStruct((1, 2, 2, 8, FF), F32),
        jax.ShapeDtypeStruct((6, 2, 1024), F32),
    )
    found = pl.pallas_call(
        kernel,
        out_shape=tuple(pltpu.VMEM(v.shape, v.dtype) for v in results),
        in_specs=[anywhere] * len(args),
        out_specs=(vmem,) * 3,
        scratch_shapes=scratch,
        compiler_params=pltpu.CompilerParams(collective_id=0, has_side_effects=True, vmem_limit_bytes=62 << 20),
    )(*args)
    grad_tokens, grad_in, grad_out_clip = pl.pallas_call(
        hand_out, out_shape=results, in_specs=[vmem] * 3, out_specs=(vmem,) * 3
    )(*(pltpu.with_memory_space_constraint(v, pltpu.VMEM) for v in found))
    return grad_tokens, grad_in, grad_out_clip.transpose(1, 0, 2)[None]


def solution(mesh):
    return jax.shard_map(
        body,
        mesh=mesh,
        in_specs=(
            P(("expert", "dp"), None),
            P(("expert", "dp"), None),
            P(("expert", "dp"), None),
            P(("expert", "dp"), None),
            P("expert", None, "dp", None),
            P("expert", None, "dp"),
            P("expert", None, None, None, None),
            P("expert", None, None, None, None),
            P("expert", None, None, None),
            P("expert", None, None, None),
        ),
        out_specs=(
            P(("expert", "dp"), None),
            P("expert", None, None, "dp", None),
            P("expert", None, None, "dp"),
        ),
        check_vma=False,
    )
```

```python
import functools

import jax
import jax.numpy as jnp
from jax import lax
from jax.experimental import pallas as pl
from jax.experimental.pallas import tpu as pltpu
from jax.sharding import PartitionSpec as P

MESH = pl.DeviceIdType.MESH
D, FF, TOK = 2048, 768, 64
WIDTH = ((640, 640, 768), (640, 768, 640), (768, 640, 640))
FIRST = ((0, 640, 1280), (0, 640, 1408), (0, 768, 1408))
BF, F32, I32 = jnp.bfloat16, jnp.float32, jnp.int32
HI = lax.Precision.HIGHEST


def dot(a, b, da, db, **kw):
    return lax.dot_general(a, b, (((da,), (db,)), ((), ())), preferred_element_type=F32, **kw)


def iota(shape, dim):
    return lax.broadcasted_iota(I32, shape, dim)


def sigmoid(v):
    return 1.0 / (1.0 + jnp.exp(-v))


def down_blocks():
    out = []
    for k in range(3):
        for block in range(8):
            rows = range(block * 32, block * 32 + 32)
            groups = {}
            for r in rows:
                groups.setdefault((3 * r + k) // 128, []).append(r - block * 32)
            out.append((k, block * 32, [(g, min(v), max(v) + 1) for g, v in sorted(groups.items())]))
    return out


def split3(v):
    high = v.astype(BF)
    rest = v - high.astype(F32)
    mid = rest.astype(BF)
    low = (rest - mid.astype(F32)).astype(BF)
    return jnp.concatenate([high, mid, low], axis=0)


def join3(v):
    n = v.shape[0] // 3
    return (v[2 * n :] + v[n : 2 * n]) + v[:n]


def nibble_order():
    return jnp.where(
        iota((FF, FF), 0) == 3 * (iota((FF, FF), 1) & 255) + (iota((FF, FF), 1) >> 8), 1.0, 0.0
    ).astype(BF)


def kernel(
    tok, go, ids, rw, cin, cout, clin, rgin, clout, rgout,
    o_tok, o_in, o_out,
    tab, t4a, t4b, t4c, g4a, g4b, g4c, pw4,
    sma, smb, smc, dma_, dmb, dmc, sxa, sxb, sxc, dxa, dxb, dxc,
    x5, d5, g5, xeb, xec, deb, dec, geb, gec,
    rma, rmb, rmc, rxa, rxb, rxc, p4s, p4t, ta, tb, tc,
    wgu, wd, upgu, logu, upo, loo, cinv, coutv, idv, rwv, clinv, rginv, cloutv, rgoutv,
    hid, ggu, fac, act, qa, qb, qc, ha, hb, hc,
    sbi, sbo, rbi, rbo,
    in_l, ag_s, ag_r, pw_s, pw_r, sl_s, sl_r, sl_l, rt_s, rt_r, rt_l, pt_s, pt_r, wt_s, wt_r, sm_s, sm_r,
):
    e, d = lax.axis_index("expert"), lax.axis_index("dp")
    z, y, x = e // 16, (e // 4) % 4, e % 4
    here = (x, y, z)
    t4, g4 = (t4a, t4b, t4c), (g4a, g4b, g4c)
    s_main, s_tail = ((sma, smb, smc), (dma_, dmb, dmc)), ((sxa, sxb, sxc), (dxa, dxb, dxc))
    xe, de, ge = (None, xeb, xec), (None, deb, dec), (None, geb, gec)
    r_main, r_tail = (rma, rmb, rmc), (rxa, rxb, rxc)
    part, got = (qa, qb, qc), (ha, hb, hc)
    cols = [[pl.ds(FIRST[t][c], WIDTH[t][c]) for c in range(3)] for t in range(3)]

    def expert_at(zz, yy, xx):
        return zz * 16 + yy * 4 + xx

    def line_peer(c, k):
        s = (here[c] + k) % 4
        return s, (expert_at(z, y, s), expert_at(z, s, x), expert_at(s, y, x))[c]

    def pieces(k):
        return [pl.ds(0, TOK)] if k != 2 else [pl.ds(0, TOK // 2), pl.ds(TOK // 2, TOK // 2)]

    def plane_peer(c, o):
        a, b = o // 4, o % 4
        u, v = ((z, y), (z, x), (y, x))[c]
        u, v = (u + a) % 4, (v + b) % 4
        return u, v, (expert_at(u, v, x), expert_at(u, y, v), expert_at(z, u, v))[c]

    def nearest(i):
        return jnp.where(i < 7, 0x8DF134C >> (4 * jnp.minimum(i, 6)), 0x6A9BE257 >> (4 * jnp.maximum(i - 7, 0))) & 15

    def main_rows(ref, t, c, u, v):
        if c == 0:
            return ref.at[u, v, :, :, cols[t][c]]
        if c == 1:
            return ref.at[u, :, v, :, cols[t][c]]
        return ref.at[pl.ds(0, 4), u, v, :, cols[t][c]]

    def tail_rows(ref, sides, t, c, u, v):
        if c == 0:
            return ref.at[4 + u // 2, (u % 2) * 2 + v // 2, pl.ds((v % 2) * 2, 2), :, cols[t][c]]
        return sides[c].at[u * 4 + v]

    def remote(src, dst, s, r, who, core):
        return pltpu.make_async_remote_copy(
            src_ref=src, dst_ref=dst, send_sem=s, recv_sem=r, device_id=(who, core), device_id_type=MESH
        )

    def wait_bytes(ref, sem):
        pltpu.make_async_copy(ref, ref, sem).wait()

    plane_me = (z * 4 + y, z * 4 + x, y * 4 + x)
    plane_uv = ((z, y), (z, x), (y, x))

    barrier = pltpu.get_barrier_semaphore()
    for c in range(3):
        for k in (2, 1, 3):
            pl.semaphore_signal(barrier, inc=1, device_id=(line_peer(c, k)[1], d), device_id_type=MESH)
    pl.semaphore_signal(barrier, inc=1, device_id=(e, 1 - d), device_id_type=MESH)

    small = [(ids, idv), (rw, rwv), (clin, clinv), (rgin, rginv), (clout, cloutv), (rgout, rgoutv), (cin, cinv), (cout, coutv)]
    loads = [pltpu.make_async_copy(src, dst, in_l.at[6 + i]) for i, (src, dst) in enumerate(small)]
    loads[0].start()
    loads[1].start()
    for c in range(3):
        pltpu.make_async_copy(tok.at[:, cols[0][c]], t4[c].at[here[c]], in_l.at[c]).start()
    for c in range(3):
        pltpu.make_async_copy(go.at[:, cols[1][c]], g4[c].at[here[c]], in_l.at[3 + c]).start()
    for load in loads[2:]:
        load.start()
    loads[0].wait()
    loads[1].wait()

    row = iota((128, TOK), 0)
    chosen = jnp.zeros((128, TOK), F32)
    weight = jnp.zeros((128, TOK), F32)
    for k in range(8):
        ident = idv[k : k + 1, :]
        chosen = chosen + jnp.where(row == ident, 1.0, 0.0)
        weight = weight + jnp.where(row == ident + 64, rwv[k : k + 1, :], 0.0)
    earlier = jnp.where(iota((TOK, TOK), 0) < iota((TOK, TOK), 1), 1.0, 0.0).astype(BF)
    before = dot(chosen.astype(BF), earlier, 1, 0)
    rank = jnp.where(chosen > 0.5, before, jnp.where(row < 64, -64.0, 0.0))
    table = rank + weight
    high = table.astype(BF).astype(F32)
    left = table - high
    mid = left.astype(BF).astype(F32)
    low = left - mid
    table = jnp.concatenate([high, jnp.concatenate([low[64:], mid[64:]], axis=0)], axis=1).astype(BF)
    plans = []
    for c in range(3):
        s, i = iota((4, 32, 128), 0), iota((4, 32, 128), 1)
        u, v = (i >> 2) & 3, i & 3
        named = (expert_at(u, v, s), expert_at(u, s, v), expert_at(s, u, v))[c] + (i >> 4) * 64
        plans.append(jnp.where(iota((4, 32, 128), 2) == named, 1.0, 0.0).reshape(128, 128))
    plans = jnp.concatenate(plans, axis=0).astype(BF)
    tab.reshape(384, 128)[...] = dot(plans, table, 1, 0).astype(BF)
    for c in range(3):
        pw4[c, here[c]] = tab[c * 4 + here[c]]

    for c in range(3):
        wait_bytes(t4[c].at[here[c]], in_l.at[c])
        wait_bytes(g4[c].at[here[c]], in_l.at[3 + c])
    pl.semaphore_wait(barrier, 10)

    for k in (2, 1, 3):
        for c in range(3):
            at, who = line_peer(c, k)
            remote(tab.at[c * 4 + at], pw4.at[c, here[c]], pw_s.at[c], pw_r.at[c], who, d).start()
    for t, q4 in enumerate((t4, g4)):
        for k in (2, 1, 3):
            for c in range(3):
                _, who = line_peer(c, k)
                for rows in pieces(k):
                    mine = q4[c].at[here[c], rows]
                    remote(mine, mine, ag_s.at[t, c], ag_r.at[t, c], who, d).start()

    for load in loads[2:]:
        load.wait()
    ends = [sigmoid(clinv[p, t]) * rginv[p, t] for p in range(2) for t in range(2)]
    ends = join3(dot(split3(jnp.concatenate(ends, axis=0)), nibble_order(), 1, 0))
    for p in range(2):
        upgu[:, p * FF : (p + 1) * FF] = ends[p * 32 : p * 32 + 16]
        logu[:, p * FF : (p + 1) * FF] = ends[p * 32 + 16 : p * 32 + 32]
    for g in range(6):
        end = sigmoid(cloutv[g]) * rgoutv[g]
        upo[g : g + 1, :] = end[0:1]
        loo[g : g + 1, :] = end[1:2]

    def dequant_in(g, carry):
        up = upgu[pl.ds(d * 8 + g, 1), :]
        lo = logu[pl.ds(d * 8 + g, 1), :]
        step = (up + lo) / 15.0
        for p in range(2):
            words = cinv[p, pl.ds(g * 128, 128), :]
            for k in range(3):
                c0 = p * FF + k * 256
                code = ((words >> (4 * k)) & 15).astype(F32)
                wgu[pl.ds(d * 1024 + g * 128, 128), c0 : c0 + 256] = (
                    code * step[:, c0 : c0 + 256] - lo[:, c0 : c0 + 256]
                ).astype(BF)
        return carry

    lax.fori_loop(0, 8, dequant_in, 0)
    half = pl.ds(pl.multiple_of(d * 1024, 1024), 1024)
    up_half, lo_half = upo[:, half], loo[:, half]
    step_half = (up_half + lo_half) / 15.0
    for k, r0, groups in down_blocks():
        code = ((coutv[r0 : r0 + 32, :] >> (4 * k)) & 15).astype(F32)
        unit = iota((32, 1024), 0)
        scale, shift = step_half[groups[0][0]][None], lo_half[groups[0][0]][None]
        for g, first, _ in groups[1:]:
            scale = jnp.where(unit >= first, step_half[g][None], scale)
            shift = jnp.where(unit >= first, lo_half[g][None], shift)
        wd[k * 256 + r0 : k * 256 + r0 + 32, half] = (code * scale - shift).astype(BF)

    other = 1 - d
    wgu_half = wgu.at[pl.ds(pl.multiple_of(d * 1024, 1024), 1024), :]
    wd_half = wd.at[:, half]
    remote(wgu_half, wgu_half, wt_s.at[0], wt_r.at[0], e, other).start()
    remote(wd_half, wd_half, wt_s.at[1], wt_r.at[1], e, other).start()

    def selector(first):
        def rows(n):
            hit = iota((16, n, 32), 2) == iota((16, n, 32), 0) + first
            return jnp.where(hit, 1.0, 0.0).reshape(16 * n, 32)

        return jnp.concatenate([rows(32), rows(16)], axis=0).astype(BF)

    first_half, second_half, either = selector(0), selector(16), selector(0) + selector(16)
    r = iota((16, 32, 256), 1)
    want_main = (r >> 3) * 16 + (r & 7) - 16 * (iota((16, 32, 256), 2) >> 6)
    r = iota((16, 16, 256), 1)
    want_tail = (r >> 2) * 16 + 8 + (r & 3) - 16 * (iota((16, 16, 256), 2) >> 6)
    wanted = jnp.concatenate([want_main.reshape(512, 256), want_tail.reshape(256, 256)], axis=0).astype(F32)

    def spread(t, src, to, first=0, last=15, ranges=(0, 1, 2)):
        def one(i, carry):
            for c in ranges:
                u, v, who = plane_peer(c, nearest(i))
                remote(src[c].at[u * 4 + v], to(c), sl_s.at[t, c], sl_r.at[t, c], who, d).start()
            return carry

        lax.fori_loop(first, last, one, 0)
        if last == 15:
            for c in ranges:
                pltpu.make_async_copy(src[c].at[plane_me[c]], to(c), sl_l.at[t, c]).start()

    above, below = [], []
    for c in range(3):
        wait_bytes(pw4.at[c, pl.ds(0, 3)], pw_r.at[c])
        heard = [pw4[c, s].astype(F32) for s in range(4)]
        above.append(jnp.concatenate([v[:, :64] for v in heard], axis=1).astype(BF))
        below.append(jnp.concatenate([v[:, 64:] for v in heard], axis=1).astype(BF))
        found = dot(first_half, above[c], 1, 0)
        p4s[c] = jnp.where(found == wanted, 1.0, 0.0).astype(BF)
    for c in range(3):
        wait_bytes(t4[c].at[pl.ds(0, 3)], ag_r.at[0, c])
        rows = dot(p4s[c, :512], t4[c][...].reshape(256, WIDTH[0][c]), 1, 0).astype(BF)
        s_main[0][c].reshape(512, WIDTH[0][c])[...] = rows
        spread(0, s_main[0], lambda c: main_rows(x5, 0, c, *plane_uv[c]), 0, 4, (c,))
    spread(0, s_main[0], lambda c: main_rows(x5, 0, c, *plane_uv[c]), 4)
    slot_weights = []
    for c in range(3):
        named = dot(either, below[c], 1, 0) + dot(second_half, above[c], 1, 0)
        slot_weights.append(jnp.sum(p4s[c].astype(F32) * named, axis=1, keepdims=True))
    for c in range(3):
        wait_bytes(g4[c].at[pl.ds(0, 3)], ag_r.at[1, c])
        rows = dot(p4s[c, :512], g4[c][...].reshape(256, WIDTH[1][c]), 1, 0)
        s_main[1][c].reshape(512, WIDTH[1][c])[...] = (slot_weights[c][:512] * rows).astype(BF)
    spread(1, s_main[1], lambda c: main_rows(d5, 1, c, *plane_uv[c]))
    for c in range(3):
        rows = dot(p4s[c, 512:], t4[c][...].reshape(256, WIDTH[0][c]), 1, 0).astype(BF)
        s_tail[0][c].reshape(256, WIDTH[0][c])[...] = rows
    spread(2, s_tail[0], lambda c: tail_rows(x5, xe, 0, c, *plane_uv[c]))
    for c in range(3):
        rows = dot(p4s[c, 512:], g4[c][...].reshape(256, WIDTH[1][c]), 1, 0)
        s_tail[1][c].reshape(256, WIDTH[1][c])[...] = (slot_weights[c][512:] * rows).astype(BF)
    spread(3, s_tail[1], lambda c: tail_rows(d5, de, 1, c, *plane_uv[c]))

    def moved(v, c):
        if c == 1:
            return (v & 0xC3) | ((v >> 2) & 0x0C) | ((v << 2) & 0x30)
        return ((v & 0x0C) << 4) | ((v & 0xF0) >> 2) | (v & 3)

    def arrived(t, src):
        for c in range(3):
            wait_bytes(src[c].at[pl.ds(0, 15)], sl_r.at[t, c])
            wait_bytes(src[c].at[0], sl_l.at[t, c])

    def order_tail(to, sides, t):
        for c in (1, 2):
            order = jnp.where(iota((256, 256), 0) == moved(iota((256, 256), 1), c), 1.0, 0.0).astype(BF)
            to.reshape(768, D)[512:768, FIRST[t][c] : FIRST[t][c] + WIDTH[t][c]] = dot(
                order, sides[c][...].reshape(256, WIDTH[t][c]), 1, 0
            ).astype(BF)

    def forward(i, carry):
        rows = pl.ds(pl.multiple_of(i * 256, 256), 256)
        token_rows = x5.reshape(768, D)[rows, :]
        pre = dot(token_rows, wgu[...], 1, 0)
        gate, up = pre[:, :FF], pre[:, FF:]
        sig = sigmoid(gate)
        silu = gate * sig
        hid[rows, :] = (silu * up).astype(BF)
        act[rows, :] = silu
        fac[rows, :] = up * sig * (1.0 + gate * (1.0 - sig))
        return carry

    def backward(i, carry):
        rows = pl.ds(pl.multiple_of(i * 256, 256), 256)
        grad_hidden = dot(d5.reshape(768, D)[rows, :], wd[...], 1, 1)
        ggu[rows, :FF] = (grad_hidden * fac[rows, :]).astype(BF)
        ggu[rows, FF:] = (grad_hidden * act[rows, :]).astype(BF)
        g5.reshape(768, D)[rows, :] = dot(ggu[rows, :], wgu[...], 1, 1).astype(BF)
        return carry

    def give_back(t, dst, rows_of):
        def one(i, carry):
            for c in range(3):
                u, v, who = plane_peer(c, nearest(i))
                remote(rows_of(c, u, v), dst[c].at[plane_me[c]], rt_s.at[t, c], rt_r.at[t, c], who, d).start()
            return carry

        lax.fori_loop(0, 15, one, 0)
        for c in range(3):
            pltpu.make_async_copy(rows_of(c, *plane_uv[c]), dst[c].at[plane_me[c]], rt_l.at[t, c]).start()

    for c in range(3):
        p4t[c] = p4s[c].T
    wait_bytes(wgu_half, wt_r.at[0])
    wait_bytes(wd_half, wt_r.at[1])
    arrived(0, s_main[0])
    lax.fori_loop(0, 2, forward, 0)
    arrived(1, s_main[1])
    lax.fori_loop(0, 2, backward, 0)
    give_back(0, r_main, lambda c, u, v: main_rows(g5, 2, c, u, v))

    arrived(2, s_tail[0])
    order_tail(x5, xe, 0)
    lax.fori_loop(2, 3, forward, 0)
    arrived(3, s_tail[1])
    order_tail(d5, de, 1)
    lax.fori_loop(2, 3, backward, 0)
    for c in (1, 2):
        order = jnp.where(moved(iota((256, 256), 0), c) == iota((256, 256), 1), 1.0, 0.0).astype(BF)
        ge[c].reshape(256, WIDTH[2][c])[...] = dot(
            order, g5.reshape(768, D)[512:768, FIRST[2][c] : FIRST[2][c] + WIDTH[2][c]], 1, 0
        ).astype(BF)
    give_back(1, r_tail, lambda c, u, v: tail_rows(g5, ge, 2, c, u, v))

    def sums_in(j, carry):
        wide = pl.ds(pl.multiple_of(j * 512, 512), 512)
        grads = dot(x5.reshape(768, D)[:, wide], ggu[...], 0, 0)
        for g in range(4):
            low = logu[pl.ds(j * 4 + g, 1), :]
            grad = grads[g * 128 : (g + 1) * 128]
            value = wgu[pl.ds(j * 512 + g * 128, 128), :].astype(F32)
            at = pl.ds((j % 2) * 4 + g, 1)
            sbi[j // 2, 0, at, :] = jnp.sum(grad * (value + low), axis=0, keepdims=True)
            sbi[j // 2, 1, at, :] = jnp.sum(grad, axis=0, keepdims=True)
        return carry

    lax.fori_loop(0, 4, sums_in, 0)
    sbi_out = sbi.at[other]
    remote(sbi_out, rbi, sm_s.at[0], sm_r.at[0], e, other).start()

    def sums_out(j, carry):
        wide = pl.ds(pl.multiple_of(j * 512, 512), 512)
        grads = dot(hid[...], d5.reshape(768, D)[:, wide], 0, 0)
        low = loo[:, wide]
        total = [[jnp.zeros((1, 512), F32)] * 6, [jnp.zeros((1, 512), F32)] * 6]
        for k, r0, groups in down_blocks():
            grad = grads[k * 256 + r0 : k * 256 + r0 + 32]
            value = wd[k * 256 + r0 : k * 256 + r0 + 32, wide].astype(F32)
            unit = iota((32, 512), 0)
            for g, first, last in groups:
                mine = grad
                if len(groups) > 1:
                    mine = jnp.where((unit >= first) & (unit < last), grad, 0.0)
                total[0][g] = total[0][g] + jnp.sum(mine * (value + low[g][None]), axis=0, keepdims=True)
                total[1][g] = total[1][g] + jnp.sum(mine, axis=0, keepdims=True)
        at = pl.ds(pl.multiple_of((j % 2) * 512, 512), 512)
        for t in range(2):
            for g in range(6):
                sbo[j // 2, t, g : g + 1, at] = total[t][g]
        return carry

    lax.fori_loop(0, 4, sums_out, 0)
    sbo_out = sbo.at[other]
    remote(sbo_out, rbo, sm_s.at[1], sm_r.at[1], e, other).start()

    wait_bytes(rbi, sm_r.at[0])
    share = pl.ds(pl.multiple_of(d * 8, 8), 8)
    upper_sum = (sbi[d, 0] + rbi[0]) / (upgu[share, :] + logu[share, :])
    lower_sum = upper_sum - (sbi[d, 1] + rbi[1])
    totals = [total[:, p * FF : (p + 1) * FF] for p in range(2) for total in (upper_sum, lower_sum)]
    plain = join3(dot(split3(jnp.concatenate(totals, axis=0)), nibble_order(), 1, 1))
    for p in range(2):
        for t in range(2):
            sig = sigmoid(clinv[p, t, share, :])
            total = plain[(p * 2 + t) * 8 : (p * 2 + t) * 8 + 8]
            o_in[0, p, t] = total * rginv[p, t, share, :] * sig * (1.0 - sig)
    wait_bytes(rbo, sm_r.at[1])
    span = upo[:, half] + loo[:, half]
    upper_out = (sbo[d, 0] + rbo[0])[:6] / span
    lower_out = upper_out - (sbo[d, 1] + rbo[1])[:6]
    for g in range(6):
        sig = sigmoid(cloutv[g, :, half])
        total = jnp.concatenate([upper_out[g : g + 1], lower_out[g : g + 1]], axis=0)
        o_out[g] = total * rgoutv[g, :, half] * sig * (1.0 - sig)

    sums = (ta, tb, tc)
    for c in range(3):
        wait_bytes(r_main[c].at[pl.ds(0, 15)], rt_r.at[0, c])
        wait_bytes(r_main[c].at[0], rt_l.at[0, c])
        sums[c][...] = dot(p4t[c, :, :512], r_main[c].reshape(512, WIDTH[2][c])[...], 1, 0)
    for c in range(3):
        wait_bytes(r_tail[c].at[pl.ds(0, 15)], rt_r.at[1, c])
        wait_bytes(r_tail[c].at[0], rt_l.at[1, c])
        total = sums[c][...] + dot(p4t[c, :, 512:], r_tail[c].reshape(256, WIDTH[2][c])[...], 1, 0)
        part[c][...] = total.astype(BF).reshape(4, TOK, WIDTH[2][c])
        for k in (2, 1, 3):
            s, who = line_peer(c, k)
            for rows in pieces(k):
                remote(part[c].at[s, rows], got[c].at[here[c], rows], pt_s.at[c], pt_r.at[c], who, d).start()
    for c in range(3):
        wait_bytes(got[c].at[pl.ds(0, 3)], pt_r.at[c])
        total = part[c][here[c]].astype(F32)
        for k in (1, 2, 3):
            s, _ = line_peer(c, k)
            total = total + got[c][s].astype(F32)
        o_tok[:, cols[2][c]] = total.astype(BF)

    for c in range(3):
        wait_bytes(pw4.at[c, pl.ds(0, 3)], pw_s.at[c])
        wait_bytes(t4[c].at[pl.ds(0, 3)], ag_s.at[0, c])
        wait_bytes(g4[c].at[pl.ds(0, 3)], ag_s.at[1, c])
        for t in range(2):
            wait_bytes(s_main[t][c].at[pl.ds(0, 15)], sl_s.at[t, c])
            wait_bytes(s_tail[t][c].at[pl.ds(0, 15)], sl_s.at[2 + t, c])
        wait_bytes(r_main[c].at[pl.ds(0, 15)], rt_s.at[0, c])
        wait_bytes(r_tail[c].at[pl.ds(0, 15)], rt_s.at[1, c])
        wait_bytes(got[c].at[pl.ds(0, 3)], pt_s.at[c])
    wait_bytes(wgu_half, wt_s.at[0])
    wait_bytes(wd_half, wt_s.at[1])
    wait_bytes(sbi_out, sm_s.at[0])
    wait_bytes(sbo_out, sm_s.at[1])


def hand_out(a, b, c, to_a, to_b, to_c, sems):
    copies = [
        pltpu.make_async_copy(src, dst, sems.at[i]) for i, (src, dst) in enumerate(((a, to_a), (b, to_b), (c, to_c)))
    ]
    for copy in copies:
        copy.start()
    for copy in copies:
        copy.wait()


def body(tokens, grad_out, expert_ids, router_weights, codes_in, codes_out, clip_in, range_in, clip_out, range_out):
    def vm(*shape, t=BF):
        return pltpu.VMEM(shape, t)

    dma = pltpu.SemaphoreType.DMA
    tok_w, slope_w, back_w = WIDTH
    scratch = [vm(12, 32, 128)]
    scratch += [vm(4, TOK, w) for w in tok_w + slope_w] + [vm(3, 4, 32, 128)]
    scratch += [vm(16, 4, 8, w) for w in tok_w + slope_w] + [vm(16, 2, 8, w) for w in tok_w + slope_w]
    scratch += [vm(6, 4, 4, 8, D)] * 3
    scratch += [vm(16, 2, 8, w) for w in tok_w[1:] + slope_w[1:] + back_w[1:]]
    scratch += [vm(16, 4, 8, w) for w in back_w] + [vm(16, 2, 8, w) for w in back_w] + [vm(3, 768, 256), vm(3, 256, 768)]
    scratch += [vm(256, w, t=F32) for w in back_w]
    scratch += [vm(D, 2 * FF), vm(FF, D), vm(16, 2 * FF, t=F32), vm(16, 2 * FF, t=F32), vm(6, D, t=F32), vm(6, D, t=F32)]
    scratch += [vm(2, 1024, 256, t=I32), vm(256, 1024, t=I32), vm(8, TOK, t=I32), vm(8, TOK, t=F32)]
    scratch += [vm(2, 2, 16, FF, t=F32)] * 2 + [vm(6, 2, D, t=F32)] * 2
    scratch += [vm(768, FF), vm(768, 2 * FF), vm(768, FF, t=F32), vm(768, FF, t=F32)]
    scratch += [vm(4, TOK, w) for w in back_w] * 2
    scratch += [vm(2, 2, 8, 2 * FF, t=F32), vm(2, 2, 8, 1024, t=F32), vm(2, 8, 2 * FF, t=F32), vm(2, 8, 1024, t=F32)]
    scratch += [dma((14,)), dma((2, 3)), dma((2, 3)), dma((3,)), dma((3,)), dma((4, 3)), dma((4, 3)), dma((4, 3))]
    scratch += [dma((2, 3)), dma((2, 3)), dma((2, 3)), dma((3,)), dma((3,)), dma((2,)), dma((2,)), dma((2,)), dma((2,))]
    args = (
        tokens, grad_out, expert_ids.T, router_weights.T, codes_in[0], codes_out[0],
        clip_in[0], range_in[0], clip_out[0].transpose(1, 0, 2), range_out[0].transpose(1, 0, 2),
    )
    vmem, anywhere = pl.BlockSpec(memory_space=pltpu.VMEM), pl.BlockSpec(memory_space=pl.ANY)
    results = (
        jax.ShapeDtypeStruct((TOK, D), BF),
        jax.ShapeDtypeStruct((1, 2, 2, 8, FF), F32),
        jax.ShapeDtypeStruct((6, 2, 1024), F32),
    )
    found = pl.pallas_call(
        kernel,
        out_shape=tuple(pltpu.VMEM(v.shape, v.dtype) for v in results),
        in_specs=[anywhere] * len(args),
        out_specs=(vmem,) * 3,
        scratch_shapes=scratch,
        compiler_params=pltpu.CompilerParams(collective_id=0, has_side_effects=True, vmem_limit_bytes=62 << 20),
    )(*args)
    grad_tokens, grad_in, grad_out_clip = pl.pallas_call(
        hand_out, out_shape=results, in_specs=[vmem] * 3, out_specs=(anywhere,) * 3, scratch_shapes=[dma((3,))]
    )(*(pltpu.with_memory_space_constraint(v, pltpu.VMEM) for v in found))
    return grad_tokens, grad_in, grad_out_clip.transpose(1, 0, 2)[None]


def solution(mesh):
    return jax.shard_map(
        body,
        mesh=mesh,
        in_specs=(
            P(("expert", "dp"), None),
            P(("expert", "dp"), None),
            P(("expert", "dp"), None),
            P(("expert", "dp"), None),
            P("expert", None, "dp", None),
            P("expert", None, "dp"),
            P("expert", None, None, None, None),
            P("expert", None, None, None, None),
            P("expert", None, None, None),
            P("expert", None, None, None),
        ),
        out_specs=(
            P(("expert", "dp"), None),
            P("expert", None, None, "dp", None),
            P("expert", None, None, "dp"),
        ),
        check_vma=False,
    )
```
